256 devices in a mesh: dp: 32 (over y, x, z_lo), cam: 8 (over z_hi, core).
Axes of the slice: x: 4, y: 4, z: 8 (z_hi: 4, z_lo: 2; z = z_hi * 2 + z_lo), core: 2. Of those that a mesh axis runs over, the one named last changes fastest.
Arguments:
- grad_out: bfloat16 [32768, 3072], P(('dp', 'cam')), may hold values from -6 to 6
- query_act: bfloat16 [32768, 2048], P(('dp', 'cam')), may hold values from -13 to 13
- key_act: bfloat16 [32768, 2048], P(('dp', 'cam')), may hold values from -13 to 13
- value_act: bfloat16 [32768, 2048], P(('dp', 'cam')), may hold values from -6 to 6
- out_proj: bfloat16 [3072, 2048], P('dp'), may hold values from -0.125 to 0.125
- view_counts: int32 [32, 4], P('dp'), may hold values from 1 to 12, 16 in all within a row
- view_slots: int32 [32, 16], P('dp'), may hold values from 0 to 15, each once within a row
Outputs:
- grad_query: bfloat16 [32768, 2048], P(('dp', 'cam'))
- grad_key: bfloat16 [32768, 2048], P(('dp', 'cam'))
- grad_value: bfloat16 [32768, 2048], P(('dp', 'cam'))
- grad_proj: float32 [3072, 2048], P('dp')
The draws below stay inside these ranges and needn't reach their ends.
Inputs may be any that keep to these rules, and one draw needn't show every extreme that they name: `view_counts`: in each group the 4 counts sum to 16, and the largest is exactly 12. `view_slots`: each row is a permutation of the group's 16 slots.
All inputs are finite; a program needn't handle non-finite values.
Results may differ from the reference program's by a relative error of at most 0.0096.
Values may be sent and summed in bfloat16 or wider, within the bound.
A program may use at most 64 MiB of HBM per device.

```python
import math
import jax
import jax.numpy as jnp
import numpy as np
from jax import lax

D = 3072
HEADS = 16
HEAD_DIM = 128
VIEW_TOK = 64
HD = 2048
GROUP = 16
OBJ = 4
MAXV = 12
TOKENS = 32768
N_DP = 32


def paired_rows(key):
    query_seed = jax.random.fold_in(key, 101)
    key_seed = jax.random.fold_in(key, 202)
    query_rows = jnp.clip(jax.random.normal(query_seed, (TOKENS, HD), jnp.float32), -4.0, 4.0)
    key_rows = jnp.clip(jax.random.normal(key_seed, (TOKENS, HD), jnp.float32), -4.0, 4.0)
    return (query_rows, key_rows)


def draw_query_act(key, part):
    return paired_rows(key)[0].astype(jnp.bfloat16)


def draw_key_act(key, part):
    return paired_rows(key)[1].astype(jnp.bfloat16)


def block_levels(rng, shape, cuts, smallest, high):
    gain = 1.0
    for dim, blocks in cuts:
        steps = jax.random.uniform(jax.random.fold_in(jax.random.fold_in(rng, 6), dim), (blocks,), jnp.float32, smallest / len(cuts), high / len(cuts))
        gain = gain * jnp.repeat(jnp.exp(steps), shape[dim] // blocks).reshape((-1,) + (1,) * (len(shape) - 1 - dim))
    return gain


def profile(number_of, total, most, lean):
    portions = [(1 << 20) // math.isqrt(grade ** lean) + 1 for grade in range(2, number_of + 1)]
    spare, holding = total - most - (number_of - 1), [1] * (number_of - 1)
    while spare > 0:
        movable = [i for i in range(number_of - 1) if holding[i] < most]
        pool, budget = sum([portions[i] for i in movable]), spare
        for i in movable:
            extra = min(most - holding[i], max(1, budget * portions[i] // pool), spare)
            holding[i] = holding[i] + extra
            spare = spare - extra
    return np.array([most] + holding)


def ragged_sizes(key, number_of, total, most, slope):
    if number_of == 2:
        one = jax.random.randint(key, (), max(1, total - most), min(most, total - 1) + 1)
        return jnp.stack([one, total - one])
    tallies = jnp.asarray(profile(number_of, total, most, slope), jnp.int32)
    couples = (number_of - 1) // 2
    donor, sink = tallies[1:1 + 2 * couples:2], tallies[2:2 + 2 * couples:2]
    room = jnp.minimum(donor - 1, most - sink)
    moved = jax.random.randint(jax.random.fold_in(key, 1), (couples,), 0, 1 << 20) % (room + 1)
    tallies = tallies.at[1:1 + 2 * couples:2].set(donor - moved).at[2:2 + 2 * couples:2].set(sink + moved)
    return tallies[jax.random.permutation(jax.random.fold_in(key, 2), number_of)]


def normal_values(stream_key, extent, width, most, cuts=(), held_as=jnp.bfloat16):
    factor_of = block_levels(stream_key, extent, cuts, -0.22, 0.18) if cuts else 1.0
    drawn = jax.random.normal(stream_key, extent, jnp.float32) * width * factor_of
    return jnp.minimum(jnp.maximum(drawn, -most), most).astype(held_as)


def setup_inputs(seed: int = 0) -> dict:
    arg_keys = jax.random.split(jax.random.key(seed), 8)
    return {
        "grad_out": normal_values(arg_keys[0], (TOKENS, D), 1.0, 6.0, ((0, 256),)),
        "query_act": draw_query_act(jax.random.fold_in(arg_keys[7], 71), 0),
        "key_act": draw_key_act(jax.random.fold_in(arg_keys[7], 71), 0),
        "value_act": normal_values(arg_keys[3], (TOKENS, HD), 1.0, 6.0, ((0, 256),)),
        "out_proj": normal_values(arg_keys[4], (D, HD), HD ** -0.5, 0.125, ((0, 32),)),
        "view_counts": jax.vmap(lambda own: ragged_sizes(own, OBJ, GROUP, MAXV, 2))(jax.random.split(arg_keys[5], N_DP)).reshape((N_DP, OBJ)).astype(jnp.int32),
        "view_slots": jax.vmap(lambda own: jax.random.permutation(own, GROUP))(jax.random.split(arg_keys[6], N_DP)).reshape((N_DP, GROUP)).astype(jnp.int32),
    }


def token_objects(counts, slots, view_tokens):
    count_ends = jnp.cumsum(counts).astype(jnp.int32)
    view_order = jnp.arange(slots.shape[0], dtype=jnp.int32)
    view_object = lax.optimization_barrier(jnp.sum((view_order[:, None] >= count_ends[None, :]).astype(jnp.int32), axis=1)).astype(jnp.int32)
    placed = slots[:, None] == view_order[None, :]
    slot_object = lax.optimization_barrier(jnp.sum(jnp.where(placed, view_object[:, None], 0), axis=0)).astype(jnp.int32)
    return jnp.repeat(slot_object, view_tokens)

def group_attention(query_group, key_group, value_group, grad_group, same_object):
    group_tokens = query_group.shape[0]
    score_scale = 1.0 / math.sqrt(HEAD_DIM)
    query_split = query_group.astype(jnp.float32).reshape(group_tokens, HEADS, HEAD_DIM)
    key_split = key_group.astype(jnp.float32).reshape(group_tokens, HEADS, HEAD_DIM)
    value_split = value_group.astype(jnp.float32).reshape(group_tokens, HEADS, HEAD_DIM)
    grad_split = grad_group.astype(jnp.float32).reshape(group_tokens, HEADS, HEAD_DIM)
    scores = jnp.einsum('qhd,khd->hqk', query_split, key_split) * score_scale
    scores = jnp.where(same_object[None, :, :], scores, -jnp.inf)
    row_max = lax.optimization_barrier(jnp.max(scores, axis=2, keepdims=True))
    exp_scores = jnp.exp(scores - row_max)
    probs = exp_scores / lax.optimization_barrier(jnp.sum(exp_scores, axis=2, keepdims=True))
    probs_bf16 = probs.astype(jnp.bfloat16)
    probs_wide = probs_bf16.astype(jnp.float32)
    attended_f32 = jnp.einsum('hqk,khd->qhd', probs_wide, value_split)
    row_delta = lax.optimization_barrier(jnp.sum(grad_split * attended_f32, axis=2))
    grad_probs = jnp.einsum('qhd,khd->hqk', grad_split, value_split)
    grad_scores = (probs * (grad_probs - jnp.transpose(row_delta)[:, :, None])).astype(jnp.bfloat16)
    grad_wide = grad_scores.astype(jnp.float32)
    grad_query = jnp.einsum('hqk,khd->qhd', grad_wide, key_split) * score_scale
    grad_key = jnp.einsum('hqk,qhd->khd', grad_wide, query_split) * score_scale
    grad_value = jnp.einsum('hqk,qhd->khd', probs_wide, grad_split)
    shape_flat = (group_tokens, HEADS * HEAD_DIM)
    return (attended_f32.reshape(shape_flat).astype(jnp.bfloat16), grad_query.reshape(shape_flat).astype(jnp.bfloat16), grad_key.reshape(shape_flat).astype(jnp.bfloat16), grad_value.reshape(shape_flat).astype(jnp.bfloat16))

def reference(grad_out, query_act, key_act, value_act, out_proj, view_counts, view_slots):
    grad_attn = jnp.dot(grad_out, out_proj, preferred_element_type=jnp.float32).astype(jnp.bfloat16)
    group_count = view_counts.shape[0]
    group_tokens = GROUP * VIEW_TOK

    def one_group(group_index):
        first_row = (group_index * group_tokens).astype(jnp.int32)
        query_group = lax.dynamic_slice_in_dim(query_act, first_row, group_tokens, 0)
        key_group = lax.dynamic_slice_in_dim(key_act, first_row, group_tokens, 0)
        value_group = lax.dynamic_slice_in_dim(value_act, first_row, group_tokens, 0)
        grad_group = lax.dynamic_slice_in_dim(grad_attn, first_row, group_tokens, 0)
        objects = token_objects(view_counts[group_index], view_slots[group_index], VIEW_TOK)
        same_object = objects[:, None] == objects[None, :]
        return group_attention(query_group, key_group, value_group, grad_group, same_object)
    attended, grad_query, grad_key, grad_value = lax.map(one_group, jnp.arange(group_count, dtype=jnp.int32))
    attended = attended.reshape(TOKENS, HD)
    grad_query = grad_query.reshape(TOKENS, HD)
    grad_key = grad_key.reshape(TOKENS, HD)
    grad_value = grad_value.reshape(TOKENS, HD)
    grad_proj = lax.dot_general(grad_out, attended, (((0,), (0,)), ((), ())), preferred_element_type=jnp.float32)
    return (grad_query, grad_key, grad_value, grad_proj)
```

```python
import math

import jax
import jax.numpy as jnp
from jax import lax
from jax.sharding import PartitionSpec as P

HEAD_DIM = 128
VIEW_TOK = 64


def token_objects(counts, slots, view_tokens):
    count_ends = jnp.cumsum(counts)
    view_order = jnp.arange(slots.shape[0], dtype=jnp.int32)
    view_object = jnp.sum((view_order[:, None] >= count_ends[None, :]).astype(jnp.int32), axis=1)
    placed = slots[:, None] == view_order[None, :]
    slot_object = jnp.sum(jnp.where(placed, view_object[:, None], 0), axis=0)
    return jnp.repeat(slot_object, view_tokens)


def head_attention(query_heads, key_heads, value_heads, grad_heads, same_object, head_dim):
    group_tokens, proj_width = query_heads.shape
    head_count = proj_width // head_dim
    score_scale = 1.0 / math.sqrt(head_dim)

    def one_head(head_index):
        first_col = head_index * head_dim
        query_one = lax.dynamic_slice_in_dim(query_heads, first_col, head_dim, 1)
        key_one = lax.dynamic_slice_in_dim(key_heads, first_col, head_dim, 1)
        value_one = lax.dynamic_slice_in_dim(value_heads, first_col, head_dim, 1)
        grad_one = lax.dynamic_slice_in_dim(grad_heads, first_col, head_dim, 1)
        scores = (
            lax.dot_general(
                query_one, key_one, (((1,), (1,)), ((), ())), preferred_element_type=jnp.float32
            )
            * score_scale
        )
        scores = jnp.where(same_object, scores, -jnp.inf)
        row_max = jnp.max(scores, axis=1, keepdims=True)
        exp_scores = jnp.exp(scores - row_max)
        probs = exp_scores / jnp.sum(exp_scores, axis=1, keepdims=True)
        probs_bf16 = probs.astype(jnp.bfloat16)
        attended_f32 = jnp.dot(probs_bf16, value_one, preferred_element_type=jnp.float32)
        row_delta = jnp.sum(grad_one.astype(jnp.float32) * attended_f32, axis=1)
        grad_probs = lax.dot_general(
            grad_one, value_one, (((1,), (1,)), ((), ())), preferred_element_type=jnp.float32
        )
        grad_scores = (probs * (grad_probs - row_delta[:, None])).astype(jnp.bfloat16)
        grad_query = jnp.dot(grad_scores, key_one, preferred_element_type=jnp.float32) * score_scale
        grad_key = (
            lax.dot_general(
                grad_scores, query_one, (((0,), (0,)), ((), ())), preferred_element_type=jnp.float32
            )
            * score_scale
        )
        grad_value = lax.dot_general(
            probs_bf16, grad_one, (((0,), (0,)), ((), ())), preferred_element_type=jnp.float32
        )
        return (
            attended_f32.astype(jnp.bfloat16),
            grad_query.astype(jnp.bfloat16),
            grad_key.astype(jnp.bfloat16),
            grad_value.astype(jnp.bfloat16),
        )

    stacked = lax.map(one_head, jnp.arange(head_count, dtype=jnp.int32))

    def flatten(per_head):
        return jnp.transpose(per_head, (1, 0, 2)).reshape(group_tokens, proj_width)

    return tuple((flatten(item) for item in stacked))


def local(grad_out, query_act, key_act, value_act, out_proj, view_counts, view_slots):
    objects = token_objects(view_counts[0], view_slots[0], VIEW_TOK)
    same_object = objects[:, None] == objects[None, :]
    cam = lax.axis_index("cam")
    width = query_act.shape[1] // lax.axis_size("cam")
    out_columns = lax.dynamic_slice_in_dim(out_proj, cam * width, width, 1)
    out_columns = lax.all_gather(out_columns, "dp", axis=0, tiled=True)
    whole_out = lax.all_gather(grad_out, "cam", axis=0, tiled=True)
    query_heads, key_heads, value_heads = (
        lax.all_to_all(query_act, "cam", split_axis=1, concat_axis=0, tiled=True),
        lax.all_to_all(key_act, "cam", split_axis=1, concat_axis=0, tiled=True),
        lax.all_to_all(value_act, "cam", split_axis=1, concat_axis=0, tiled=True),
    )
    grad_heads = jnp.dot(whole_out, out_columns, preferred_element_type=jnp.float32).astype(
        jnp.bfloat16
    )
    attended, grad_query, grad_key, grad_value = head_attention(
        query_heads, key_heads, value_heads, grad_heads, same_object, HEAD_DIM
    )
    partial = lax.dot_general(
        whole_out, attended, (((0,), (0,)), ((), ())), preferred_element_type=jnp.float32
    ).astype(jnp.bfloat16)
    dp = lax.axis_size("dp")
    rows = partial.shape[0] // dp
    pieces = lax.all_to_all(partial, "dp", split_axis=0, concat_axis=0, tiled=True)
    partial_rows = jnp.sum(pieces.reshape(dp, rows, width).astype(jnp.float32), axis=0)
    grad_proj = lax.all_gather(partial_rows, "cam", axis=1, tiled=True)
    grad_query, grad_key, grad_value = (
        lax.all_to_all(grad_query, "cam", split_axis=0, concat_axis=1, tiled=True),
        lax.all_to_all(grad_key, "cam", split_axis=0, concat_axis=1, tiled=True),
        lax.all_to_all(grad_value, "cam", split_axis=0, concat_axis=1, tiled=True),
    )
    return (grad_query, grad_key, grad_value, grad_proj)


def solution(mesh):
    in_specs = (
        P(("dp", "cam"), None),
        P(("dp", "cam"), None),
        P(("dp", "cam"), None),
        P(("dp", "cam"), None),
        P("dp", None),
        P("dp", None),
        P("dp", None),
    )
    out_specs = (
        P(("dp", "cam"), None),
        P(("dp", "cam"), None),
        P(("dp", "cam"), None),
        P("dp", None),
    )
    return jax.shard_map(local, mesh=mesh, in_specs=in_specs, out_specs=out_specs, check_vma=False)
```

```python
import functools
import math

import jax
import jax.numpy as jnp
from jax import lax
from jax.experimental import pallas as pl
from jax.experimental.pallas import tpu as pltpu
from jax.sharding import PartitionSpec as P

HEAD_DIM = 128
VIEW_TOK = 64
HEADS_HERE = 2
BF16 = jnp.bfloat16
F32 = jnp.float32
MESH = pl.DeviceIdType.MESH


def slot_objects(counts, slots):
    count_ends = jnp.cumsum(counts)
    view_order = jnp.arange(slots.shape[0], dtype=jnp.int32)
    view_object = jnp.sum((view_order[:, None] >= count_ends[None, :]).astype(jnp.int32), axis=1)
    placed = slots[:, None] == view_order[None, :]
    return jnp.sum(jnp.where(placed, view_object[:, None], 0), axis=0)


def dot(a, b, contract):
    return lax.dot_general(a, b, ((contract[:1], contract[1:]), ((), ())), preferred_element_type=F32)


def kernel(
    dims,
    slot_obj,
    key_obj,
    g_in,
    q_in,
    k_in,
    v_in,
    w_in,
    dq_out,
    dk_out,
    dv_out,
    gp_out,
    g_all,
    w_all,
    qkv,
    qkv_relay,
    probs,
    att,
    dk_acc,
    dv_acc,
    d_send,
    d_relay,
    gp_acc,
    gp_send,
    gp_recv,
    gp_sum,
    gp_pair,
    gp_land,
    g_recv_sem,
    g_send_sem,
    g_fwd_sem,
    w_recv_sem,
    w_send_sem,
    w_fwd_sem,
    qkv_recv_sem,
    qkv_send_sem,
    relay_recv_sem,
    relay_fwd_sem,
    d_recv_sem,
    d_send_sem,
    d_relay_sem,
    d_fwd_sem,
    rs_send_sem,
    rs_recv_sem,
    pair_sem,
    land_send_sem,
    land_recv_sem,
):
    planes, rows, width, piece = dims
    half = rows // 2
    chip_rows = 2 * rows
    tokens = 8 * rows
    scale = 1.0 / math.sqrt(HEAD_DIM)
    dp = lax.axis_index("dp")
    cam = lax.axis_index("cam")
    spot, z_lo = dp // 2, dp % 2
    pair = spot * 2 + (1 - z_lo)
    chip, core = cam // 2, cam % 2
    ahead, behind, across = (chip + 1) % 4, (chip + 3) % 4, (chip + 2) % 4
    sibling = chip * 2 + (1 - core)
    outs = (dq_out, dk_out, dv_out)
    ins = (q_in, k_in, v_in)

    def block(index):
        return pl.ds(pl.multiple_of(index * rows, rows), rows)

    def cols(index):
        return pl.ds(pl.multiple_of(index * width, width), width)

    def remote(src, dst, send, recv, **where):
        return pltpu.make_async_remote_copy(
            src_ref=src, dst_ref=dst, send_sem=send, recv_sem=recv, device_id=where, device_id_type=MESH
        )

    def arrived(ref, sem):
        pltpu.make_async_copy(ref, ref, sem).wait()

    def in_plane(step):
        return (spot + step) % planes

    barrier = pltpu.get_barrier_semaphore()

    @pl.loop(1, planes)
    def _(step):
        pl.semaphore_signal(barrier, inc=1, device_id={"dp": in_plane(step) * 2 + z_lo}, device_id_type=MESH)

    pl.semaphore_signal(barrier, inc=1, device_id={"dp": pair}, device_id_type=MESH)

    @pl.loop(1, 8)
    def _(step):
        pl.semaphore_signal(barrier, inc=1, device_id={"cam": (cam + step) % 8}, device_id_type=MESH)

    pl.semaphore_wait(barrier, planes + 7)

    def qkv_copy(j, dst_cam, slot):
        return remote(
            ins[j].at[:, cols(dst_cam)],
            qkv.at[j, block(cam), :],
            qkv_send_sem.at[slot, j],
            qkv_recv_sem.at[cam, j],
            cam=dst_cam,
        )

    def qkv_far(j, way):
        return remote(
            ins[j].at[:, cols(across * 2 + way)],
            qkv_relay.at[way, j],
            qkv_send_sem.at[5 + way, j],
            relay_recv_sem.at[way, j],
            cam=(ahead, behind)[way] * 2 + core,
        )

    def qkv_forward(j, way):
        source = (behind, ahead)[way] * 2 + core
        return remote(
            qkv_relay.at[way, j],
            qkv.at[j, block(source), :],
            relay_fwd_sem.at[way, j],
            qkv_recv_sem.at[source, j],
            cam=(ahead, behind)[way] * 2 + way,
        )

    near = (ahead * 2, behind * 2, ahead * 2 + 1, behind * 2 + 1, sibling)
    for j in range(3):
        for way in range(2):
            qkv_far(j, way).start()
        for slot in range(5):
            qkv_copy(j, near[slot], slot).start()
        pltpu.make_async_copy(
            ins[j].at[:, cols(cam)], qkv.at[j, block(cam), :], qkv_recv_sem.at[cam, j]
        ).start()

    def w_rows(index):
        return pl.ds(pl.multiple_of(index * piece, piece), piece)

    def w_copy(dst_dp, sem):
        return remote(w_in.at[:, cols(cam)], w_all.at[w_rows(dp), :], sem, w_recv_sem.at[dp], dp=dst_dp)

    def w_forward(step):
        return remote(
            w_all.at[w_rows(pair), :],
            w_all.at[w_rows(pair), :],
            w_fwd_sem.at[step],
            w_recv_sem.at[pair],
            dp=in_plane(step) * 2 + z_lo,
        )

    w_copy(pair, w_send_sem.at[0]).start()
    pltpu.make_async_copy(w_in.at[:, cols(cam)], w_all.at[w_rows(dp), :], w_recv_sem.at[dp]).start()

    @pl.loop(1, planes)
    def _(step):
        w_copy(in_plane(step) * 2 + z_lo, w_send_sem.at[step]).start()

    def g_part(index, part):
        return pl.ds(pl.multiple_of(index * rows + part * half, half), half)

    def g_own(part, slot, dst_cam):
        return remote(
            g_in.at[part * half : (part + 1) * half, :],
            g_all.at[g_part(cam, part), :],
            g_send_sem.at[slot, part],
            g_recv_sem.at[cam, part],
            cam=dst_cam,
        )

    def g_pass(source, part, sem, dst_cam):
        here = g_all.at[g_part(source, part), :]
        return remote(here, here, sem, g_recv_sem.at[source, part], cam=dst_cam)

    def g_local(part):
        return pltpu.make_async_copy(
            g_in.at[part * half : (part + 1) * half, :],
            g_all.at[g_part(cam, part), :],
            g_recv_sem.at[cam, part],
        )

    def g_wait(source, part):
        arrived(g_all.at[g_part(source, part), :], g_recv_sem.at[source, part])

    g_near = (ahead * 2 + core, behind * 2 + core, sibling)

    def g_start():
        for part in range(2):
            g_own(part, 0, g_near[0]).start()
            g_own(1 - part, 1, g_near[1]).start()
            g_own(part, 2, g_near[2]).start()
            g_local(part).start()

    g_start()

    arrived(w_all.at[w_rows(pair), :], w_recv_sem.at[pair])

    @pl.loop(1, planes)
    def _(step):
        w_forward(step).start()

    for j in range(3):
        for way in range(2):
            arrived(qkv_relay.at[way, j], relay_recv_sem.at[way, j])
            qkv_forward(j, way).start()

    for j in range(3):

        @pl.loop(0, 8)
        def _(source):
            arrived(qkv.at[j, block(source), :], qkv_recv_sem.at[source, j])

    dk_acc[...] = jnp.zeros_like(dk_acc)
    dv_acc[...] = jnp.zeros_like(dv_acc)
    gp_acc[...] = jnp.zeros_like(gp_acc)

    @pl.loop(0, 8)
    def _(r):
        here = block(r)
        row = lax.broadcasted_iota(jnp.int32, (rows, 1), 0)
        row_obj = jnp.where(row < VIEW_TOK, slot_obj[r * 2], slot_obj[r * 2 + 1])
        same = row_obj == key_obj[...]
        for i in range(HEADS_HERE):
            head = slice(i * HEAD_DIM, (i + 1) * HEAD_DIM)
            scores = dot(qkv[0, here, head], qkv[1, :, head], (1, 1)) * scale
            scores = jnp.where(same, scores, -jnp.inf)
            exps = jnp.exp(scores - jnp.max(scores, axis=1, keepdims=True))
            p = exps * (1.0 / jnp.sum(exps, axis=1, keepdims=True))
            probs[i, here, :] = p
            att[here, head] = dot(p.astype(BF16), qkv[2, :, head], (1, 0))

    @pl.loop(0, planes * 2)
    def _(source):
        @pl.when(source != pair)
        def _():
            arrived(w_all.at[w_rows(source), :], w_recv_sem.at[source])

    def d_direct(j, dst_cam, slot):
        return remote(
            d_send.at[j, block(dst_cam), :],
            outs[j].at[:, cols(cam)],
            d_send_sem.at[slot, j],
            d_recv_sem.at[cam, j],
            cam=dst_cam,
        )

    def d_far(j, way):
        return remote(
            d_send.at[j, block(across * 2 + way), :],
            d_relay.at[way, j],
            d_send_sem.at[5 + way, j],
            d_relay_sem.at[way, j],
            cam=(ahead, behind)[way] * 2 + core,
        )

    def d_forward(j, way):
        source = (behind, ahead)[way] * 2 + core
        return remote(
            d_relay.at[way, j],
            outs[j].at[:, cols(source)],
            d_fwd_sem.at[way, j],
            d_recv_sem.at[source, j],
            cam=(ahead, behind)[way] * 2 + way,
        )

    def d_local(j):
        return pltpu.make_async_copy(
            d_send.at[j, block(cam), :], outs[j].at[:, cols(cam)], d_recv_sem.at[cam, j]
        )

    def g_tile(j):
        return pl.ds(pl.multiple_of(j * 4 * piece, 128), 4 * piece)

    @pl.loop(0, 4)
    def _(t):
        step = jnp.where(t == 0, 0, jnp.where(t == 1, 3, jnp.where(t == 2, 1, 2)))
        c = (chip + step) % 4

        @pl.when(t == 1)
        def _():
            back, front = behind * 2 + core, ahead * 2 + core
            g_wait(back, 0)
            g_pass(back, 0, g_fwd_sem.at[0, 0], front).start()
            g_pass(back, 0, g_fwd_sem.at[1, 0], sibling).start()
            g_wait(front, 1)
            g_pass(front, 1, g_fwd_sem.at[0, 1], back).start()
            g_pass(front, 1, g_fwd_sem.at[2, 1], sibling).start()
            g_wait(back, 1)
            g_pass(back, 1, g_fwd_sem.at[1, 1], sibling).start()
            g_wait(front, 0)
            g_pass(front, 0, g_fwd_sem.at[2, 0], sibling).start()

        @pl.when(t == 3)
        def _():
            for part in range(2):
                g_wait(across * 2 + core, part)
                g_pass(across * 2 + core, part, g_fwd_sem.at[3, part], sibling).start()

        @pl.when(t == 0)
        def _():
            for part in range(2):
                g_wait(cam, part)

        for part in range(2):
            g_wait(c * 2 + 1 - core, part)

        here = pl.ds(pl.multiple_of(c * chip_rows, chip_rows), chip_rows)
        grad_att = dot(g_all[here, :], w_all[...], (1, 0)).astype(BF16)
        for i in range(HEADS_HERE):
            head = slice(i * HEAD_DIM, (i + 1) * HEAD_DIM)
            go = grad_att[:, head]
            p = probs[i, here, :]
            delta = jnp.sum(go.astype(F32) * att[here, head], axis=1, keepdims=True)
            ds = (p * (dot(go, qkv[2, :, head], (1, 1)) - delta)).astype(BF16)
            d_send[0, here, head] = (dot(ds, qkv[1, :, head], (1, 0)) * scale).astype(BF16)
            dk_acc[:, head] += dot(ds, qkv[0, here, head], (0, 0))
            dv_acc[:, head] += dot(p.astype(BF16), go, (0, 0))

        @pl.when(t == 0)
        def _():
            d_local(0).start()
            d_direct(0, sibling, 4).start()

        @pl.when(t == 1)
        def _():
            d_direct(0, behind * 2, 1).start()
            d_direct(0, behind * 2 + 1, 3).start()

        @pl.when(t == 2)
        def _():
            d_direct(0, ahead * 2, 0).start()
            d_direct(0, ahead * 2 + 1, 2).start()

        @pl.when(t < 3)
        def _():
            att_here = att[here, :].astype(BF16)

            @pl.loop(0, planes // 2)
            def _(j):
                gp_acc[g_tile(j), :] += dot(g_all[here, g_tile(j)], att_here, (0, 0))

    d_send[1] = (dk_acc[...] * scale).astype(BF16)
    d_send[2] = dv_acc[...].astype(BF16)
    for j in range(3):
        for way in range(2):
            d_far(j, way).start()
    for j in range(1, 3):
        for slot in range(5):
            d_direct(j, near[slot], slot).start()
        d_local(j).start()

    def two(index):
        return pl.ds(pl.multiple_of(index * 2 * piece, 2 * piece), 2 * piece)

    def rs_copy(peer):
        return remote(
            gp_send.at[two(peer), :],
            gp_recv.at[spot],
            rs_send_sem.at[peer],
            rs_recv_sem.at[spot],
            dp=peer * 2 + z_lo,
        )

    last = pl.ds(pl.multiple_of(across * chip_rows, chip_rows), chip_rows)
    att_last = att[last, :].astype(BF16)

    @pl.loop(0, planes // 2)
    def _(jj):
        j = (spot // 2 + jj) % (planes // 2)
        total = gp_acc[g_tile(j), :] + dot(g_all[last, g_tile(j)], att_last, (0, 0))
        gp_acc[g_tile(j), :] = total
        gp_send[g_tile(j), :] = total.astype(BF16)
        for side in range(2):
            peer = j * 2 + side

            @pl.when(peer != spot)
            def _():
                rs_copy(peer).start()

    for j in range(3):
        for way in range(2):
            arrived(d_relay.at[way, j], d_relay_sem.at[way, j])
            d_forward(j, way).start()

    gp_sum[...] = gp_acc[two(spot), :]

    @pl.loop(1, planes)
    def _(step):
        peer = (spot + planes - step) % planes
        arrived(gp_recv.at[peer], rs_recv_sem.at[peer])
        gp_sum[...] += gp_recv[peer].astype(F32)

    def own_half(side):
        return pl.ds(pl.multiple_of(side * piece, piece), piece)

    pair_copy = remote(
        gp_sum.at[own_half(1 - z_lo), :], gp_pair, pair_sem.at[0], pair_sem.at[1], dp=pair
    )
    pair_copy.start()
    pair_copy.wait()
    gp_land[cam] = (gp_sum[own_half(z_lo), :] + gp_pair[...]).astype(BF16)

    def land_copy(step):
        return remote(
            gp_land.at[cam],
            gp_land.at[cam],
            land_send_sem.at[step],
            land_recv_sem.at[cam],
            cam=(cam + step) % 8,
        )

    @pl.loop(1, 8)
    def _(step):
        land_copy(step).start()

    @pl.loop(1, 8)
    def _(step):
        source = (cam + 8 - step) % 8
        arrived(gp_land.at[source], land_recv_sem.at[source])

    for source in range(8):
        gp_out[:, source * width : (source + 1) * width] = gp_land[source].astype(F32)

    for j in range(3):

        @pl.loop(0, 8)
        def _(source):
            arrived(outs[j].at[:, cols(source)], d_recv_sem.at[source, j])

    for j in range(3):
        for slot in range(5):
            qkv_copy(j, near[slot], slot).wait_send()
            d_direct(j, near[slot], slot).wait_send()
        for way in range(2):
            qkv_far(j, way).wait_send()
            qkv_forward(j, way).wait_send()
            d_far(j, way).wait_send()
            d_forward(j, way).wait_send()
    w_copy(pair, w_send_sem.at[0]).wait_send()

    @pl.loop(1, planes)
    def _(step):
        w_copy(in_plane(step) * 2 + z_lo, w_send_sem.at[step]).wait_send()
        w_forward(step).wait_send()
        rs_copy(in_plane(step)).wait_send()

    for part in range(2):
        for slot in range(3):
            g_own(part, slot, g_near[slot]).wait_send()
        for slot in range(4):
            g_pass(cam, part, g_fwd_sem.at[slot, part], sibling).wait_send()

    @pl.loop(1, 8)
    def _(step):
        land_copy(step).wait_send()


def local(grad_out, query_act, key_act, value_act, out_proj, view_counts, view_slots):
    rows, model = grad_out.shape
    devices_dp = lax.axis_size("dp")
    planes = devices_dp // 2
    piece = out_proj.shape[0]
    width = query_act.shape[1] // 8
    tokens = rows * 8
    slot_obj = slot_objects(view_counts[0], view_slots[0])
    key_obj = jnp.repeat(slot_obj, VIEW_TOK)[None, :]
    dims = (planes, rows, width, piece)
    any_spec = pl.BlockSpec(memory_space=pl.ANY)
    dma = pltpu.SemaphoreType.DMA
    gradient = jax.ShapeDtypeStruct(query_act.shape, BF16)
    return pl.pallas_call(
        functools.partial(kernel, dims),
        out_shape=(gradient, gradient, gradient, jax.ShapeDtypeStruct((piece, width * 8), F32)),
        in_specs=[pl.BlockSpec(memory_space=pltpu.SMEM), pl.BlockSpec(memory_space=pltpu.VMEM)]
        + [any_spec] * 5,
        out_specs=(any_spec, any_spec, any_spec, pl.BlockSpec(memory_space=pltpu.VMEM)),
        scratch_shapes=[
            pltpu.VMEM((tokens, model), BF16),
            pltpu.VMEM((model, width), BF16),
            pltpu.VMEM((3, tokens, width), BF16),
            pltpu.VMEM((2, 3, rows, width), BF16),
            pltpu.VMEM((HEADS_HERE, tokens, tokens), F32),
            pltpu.VMEM((tokens, width), F32),
            pltpu.VMEM((tokens, width), F32),
            pltpu.VMEM((tokens, width), F32),
            pltpu.VMEM((3, tokens, width), BF16),
            pltpu.VMEM((2, 3, rows, width), BF16),
            pltpu.VMEM((model, width), F32),
            pltpu.VMEM((model, width), BF16),
            pltpu.VMEM((planes, 2 * piece, width), BF16),
            pltpu.VMEM((2 * piece, width), F32),
            pltpu.VMEM((piece, width), F32),
            pltpu.VMEM((8, piece, width), BF16),
            dma((8, 2)),
            dma((3, 2)),
            dma((4, 2)),
            dma((devices_dp,)),
            dma((planes,)),
            dma((planes,)),
            dma((8, 3)),
            dma((7, 3)),
            dma((2, 3)),
            dma((2, 3)),
            dma((8, 3)),
            dma((7, 3)),
            dma((2, 3)),
            dma((2, 3)),
            dma((planes,)),
            dma((planes,)),
            dma((2,)),
            dma((8,)),
            dma((8,)),
        ],
        compiler_params=pltpu.CompilerParams(
            collective_id=0, has_side_effects=True, vmem_limit_bytes=60 * 1024 * 1024
        ),
        name="group_backward",
    )(slot_obj, key_obj, grad_out, query_act, key_act, value_act, out_proj)


def solution(mesh):
    rows = P(("dp", "cam"), None)
    in_specs = (rows, rows, rows, rows, P("dp", None), P("dp", None), P("dp", None))
    out_specs = (rows, rows, rows, P("dp", None))
    return jax.shard_map(local, mesh=mesh, in_specs=in_specs, out_specs=out_specs, check_vma=False)
```

```python
import functools
import math

import jax
import jax.numpy as jnp
from jax import lax
from jax.experimental import pallas as pl
from jax.experimental.pallas import tpu as pltpu
from jax.sharding import PartitionSpec as P

HEAD_DIM = 128
VIEW_TOK = 64
HEADS_HERE = 2
BF16 = jnp.bfloat16
F32 = jnp.float32
MESH = pl.DeviceIdType.MESH


def dot(a, b, contract):
    return lax.dot_general(a, b, ((contract[:1], contract[1:]), ((), ())), preferred_element_type=F32)


def kernel(
    dims,
    counts,
    slots,
    g_in,
    q_in,
    k_in,
    v_in,
    w_in,
    dq_out,
    dk_out,
    dv_out,
    land_out,
    g_all,
    w_all,
    qkv,
    probs,
    att,
    dk_acc,
    dv_acc,
    d_send,
    gp_acc,
    gp_send,
    gp_recv,
    gp_sum,
    gp_pair,
    gp_last,
    slot_obj,
    key_obj,
    g_recv_sem,
    g_send_sem,
    g_fwd_sem,
    w_recv_sem,
    w_send_sem,
    w_fwd_sem,
    qkv_recv_sem,
    qkv_send_sem,
    d_recv_sem,
    d_send_sem,
    rs_send_sem,
    rs_recv_sem,
    pair_sem,
    land_send_sem,
    land_recv_sem,
):
    planes, rows, width, piece = dims
    half = rows // 2
    chip_rows = 2 * rows
    tokens = 8 * rows
    scale = 1.0 / math.sqrt(HEAD_DIM)
    dp = lax.axis_index("dp")
    cam = lax.axis_index("cam")
    spot, z_lo = dp // 2, dp % 2
    pair = spot * 2 + (1 - z_lo)
    chip, core = cam // 2, cam % 2
    ahead, behind, across = (chip + 1) % 4, (chip + 3) % 4, (chip + 2) % 4
    sibling = chip * 2 + (1 - core)
    outs = (dq_out, dk_out, dv_out)
    ins = (q_in, k_in, v_in)

    def block(index):
        return pl.ds(pl.multiple_of(index * rows, rows), rows)

    def cols(index):
        return pl.ds(pl.multiple_of(index * width, width), width)

    def remote(src, dst, send, recv, **where):
        return pltpu.make_async_remote_copy(
            src_ref=src, dst_ref=dst, send_sem=send, recv_sem=recv, device_id=where, device_id_type=MESH
        )

    def arrived(ref, sem):
        pltpu.make_async_copy(ref, ref, sem).wait()

    def in_plane(step):
        return (spot + step) % planes

    barrier = pltpu.get_barrier_semaphore()

    @pl.loop(1, planes)
    def _(step):
        pl.semaphore_signal(barrier, inc=1, device_id={"dp": in_plane(step) * 2 + z_lo}, device_id_type=MESH)

    pl.semaphore_signal(barrier, inc=1, device_id={"dp": pair}, device_id_type=MESH)

    @pl.loop(1, 8)
    def _(step):
        pl.semaphore_signal(barrier, inc=1, device_id={"cam": (cam + step) % 8}, device_id_type=MESH)

    pl.semaphore_wait(barrier, planes + 7)

    def qkv_copy(j, dst_cam, slot):
        return remote(
            ins[j].at[:, cols(dst_cam)],
            qkv.at[j, block(cam), :],
            qkv_send_sem.at[slot, j],
            qkv_recv_sem.at[cam, j],
            cam=dst_cam,
        )

    others = (across * 2, across * 2 + 1, ahead * 2, behind * 2, ahead * 2 + 1, behind * 2 + 1, sibling)
    for j in range(3):
        for slot in range(7):
            qkv_copy(j, others[slot], slot).start()
        pltpu.make_async_copy(
            ins[j].at[:, cols(cam)], qkv.at[j, block(cam), :], qkv_recv_sem.at[cam, j]
        ).start()

    def w_rows(index):
        return pl.ds(pl.multiple_of(index * piece, piece), piece)

    def w_copy(dst_dp, sem):
        return remote(w_in.at[:, cols(cam)], w_all.at[w_rows(dp), :], sem, w_recv_sem.at[dp], dp=dst_dp)

    def w_forward(step):
        return remote(
            w_all.at[w_rows(pair), :],
            w_all.at[w_rows(pair), :],
            w_fwd_sem.at[step],
            w_recv_sem.at[pair],
            dp=in_plane(step) * 2 + z_lo,
        )

    w_copy(pair, w_send_sem.at[0]).start()
    pltpu.make_async_copy(w_in.at[:, cols(cam)], w_all.at[w_rows(dp), :], w_recv_sem.at[dp]).start()

    @pl.loop(1, planes)
    def _(step):
        w_copy(in_plane(step) * 2 + z_lo, w_send_sem.at[step]).start()

    def g_part(index, part):
        return pl.ds(pl.multiple_of(index * rows + part * half, half), half)

    def g_own(part, slot, dst_cam):
        return remote(
            g_in.at[part * half : (part + 1) * half, :],
            g_all.at[g_part(cam, part), :],
            g_send_sem.at[slot, part],
            g_recv_sem.at[cam, part],
            cam=dst_cam,
        )

    def g_pass(source, part, sem, dst_cam):
        here = g_all.at[g_part(source, part), :]
        return remote(here, here, sem, g_recv_sem.at[source, part], cam=dst_cam)

    def g_local(part):
        return pltpu.make_async_copy(
            g_in.at[part * half : (part + 1) * half, :],
            g_all.at[g_part(cam, part), :],
            g_recv_sem.at[cam, part],
        )

    def g_wait(source, part):
        arrived(g_all.at[g_part(source, part), :], g_recv_sem.at[source, part])

    g_near = (ahead * 2 + core, behind * 2 + core, sibling)

    def g_start():
        for part in range(2):
            g_own(part, 0, g_near[0]).start()
            g_own(1 - part, 1, g_near[1]).start()
            g_own(part, 2, g_near[2]).start()
            g_local(part).start()


    ends = [counts[0, 0]]
    for o in range(1, counts.shape[1]):
        ends.append(ends[-1] + counts[0, o])
    views = slots.shape[1]
    view_obj = [sum((v >= end).astype(jnp.int32) for end in ends) for v in range(views)]

    @pl.loop(0, views)
    def _(s):
        found = jnp.int32(0)
        for v in range(views):
            found = found + jnp.where(slots[0, v] == s, view_obj[v], 0)
        slot_obj[s] = found

    lane_slot = lax.broadcasted_iota(jnp.int32, (1, tokens), 1) // VIEW_TOK
    lane_obj = jnp.zeros((1, tokens), jnp.int32)
    for s in range(views):
        lane_obj = jnp.where(lane_slot == s, slot_obj[s], lane_obj)
    key_obj[...] = lane_obj
    dk_acc[...] = jnp.zeros_like(dk_acc)
    dv_acc[...] = jnp.zeros_like(dv_acc)
    gp_acc[...] = jnp.zeros_like(gp_acc)

    arrived(w_all.at[w_rows(pair), :], w_recv_sem.at[pair])

    @pl.loop(1, planes)
    def _(step):
        w_forward(step).start()

    for j in range(3):

        @pl.loop(0, 8)
        def _(source):
            arrived(qkv.at[j, block(source), :], qkv_recv_sem.at[source, j])

    g_start()


    @pl.loop(0, 8)
    def _(r):
        here = block(r)
        row = lax.broadcasted_iota(jnp.int32, (rows, 1), 0)
        row_obj = jnp.where(row < VIEW_TOK, slot_obj[r * 2], slot_obj[r * 2 + 1])
        same = row_obj == key_obj[...]
        for i in range(HEADS_HERE):
            head = slice(i * HEAD_DIM, (i + 1) * HEAD_DIM)
            scores = dot(qkv[0, here, head], qkv[1, :, head], (1, 1)) * scale
            scores = jnp.where(same, scores, -jnp.inf)
            exps = jnp.exp(scores - jnp.max(scores, axis=1, keepdims=True))
            p = exps * (1.0 / jnp.sum(exps, axis=1, keepdims=True))
            probs[i, here, :] = p
            att[here, head] = dot(p.astype(BF16), qkv[2, :, head], (1, 0))

    @pl.loop(0, planes * 2)
    def _(source):
        @pl.when(source != pair)
        def _():
            arrived(w_all.at[w_rows(source), :], w_recv_sem.at[source])

    def d_direct(j, dst_cam, slot):
        return remote(
            d_send.at[j, block(dst_cam), :],
            outs[j].at[:, cols(cam)],
            d_send_sem.at[slot, j],
            d_recv_sem.at[cam, j],
            cam=dst_cam,
        )

    def d_local(j):
        return pltpu.make_async_copy(
            d_send.at[j, block(cam), :], outs[j].at[:, cols(cam)], d_recv_sem.at[cam, j]
        )

    def g_tile(j):
        return pl.ds(pl.multiple_of(j * 4 * piece, 128), 4 * piece)

    @pl.loop(0, 4)
    def _(t):
        step = jnp.where(t == 0, 0, jnp.where(t == 1, 3, jnp.where(t == 2, 1, 2)))
        c = (chip + step) % 4

        @pl.when(t == 1)
        def _():
            back, front = behind * 2 + core, ahead * 2 + core
            g_wait(back, 0)
            g_pass(back, 0, g_fwd_sem.at[0, 0], front).start()
            g_pass(back, 0, g_fwd_sem.at[1, 0], sibling).start()
            g_wait(front, 1)
            g_pass(front, 1, g_fwd_sem.at[0, 1], back).start()
            g_pass(front, 1, g_fwd_sem.at[2, 1], sibling).start()
            g_wait(back, 1)
            g_pass(back, 1, g_fwd_sem.at[1, 1], sibling).start()
            g_wait(front, 0)
            g_pass(front, 0, g_fwd_sem.at[2, 0], sibling).start()

        @pl.when(t == 3)
        def _():
            for part in range(2):
                g_wait(across * 2 + core, part)
                g_pass(across * 2 + core, part, g_fwd_sem.at[3, part], sibling).start()

        @pl.when(t == 0)
        def _():
            for part in range(2):
                g_wait(cam, part)

        for part in range(2):
            g_wait(c * 2 + 1 - core, part)

        here = pl.ds(pl.multiple_of(c * chip_rows, chip_rows), chip_rows)
        grad_att = dot(g_all[here, :], w_all[...], (1, 0)).astype(BF16)
        for i in range(HEADS_HERE):
            head = slice(i * HEAD_DIM, (i + 1) * HEAD_DIM)
            go = grad_att[:, head]
            p = probs[i, here, :]
            delta = jnp.sum(go.astype(F32) * att[here, head], axis=1, keepdims=True)
            ds = (p * (dot(go, qkv[2, :, head], (1, 1)) - delta)).astype(BF16)
            d_send[0, here, head] = (dot(ds, qkv[1, :, head], (1, 0)) * scale).astype(BF16)
            dk_acc[:, head] += dot(ds, qkv[0, here, head], (0, 0))
            dv_acc[:, head] += dot(p.astype(BF16), go, (0, 0))

        @pl.when(t == 0)
        def _():
            d_local(0).start()
            d_direct(0, sibling, 6).start()

        @pl.when(t == 1)
        def _():
            d_direct(0, behind * 2, 3).start()
            d_direct(0, behind * 2 + 1, 5).start()

        @pl.when(t == 2)
        def _():
            d_direct(0, ahead * 2, 2).start()
            d_direct(0, ahead * 2 + 1, 4).start()

        @pl.when(t < 3)
        def _():
            att_here = att[here, :].astype(BF16)

            @pl.loop(0, planes // 2)
            def _(j):
                gp_acc[g_tile(j), :] += dot(g_all[here, g_tile(j)], att_here, (0, 0))

    d_send[1] = (dk_acc[...] * scale).astype(BF16)
    d_send[2] = dv_acc[...].astype(BF16)
    for j in range(3):
        for slot in range(2 if j == 0 else 7):
            d_direct(j, others[slot], slot).start()
        if j > 0:
            d_local(j).start()

    def two(index):
        return pl.ds(pl.multiple_of(index * 2 * piece, 2 * piece), 2 * piece)

    def rs_copy(peer):
        return remote(
            gp_send.at[two(peer), :],
            gp_recv.at[spot],
            rs_send_sem.at[peer],
            rs_recv_sem.at[spot],
            dp=peer * 2 + z_lo,
        )

    last = pl.ds(pl.multiple_of(across * chip_rows, chip_rows), chip_rows)
    att_last = att[last, :].astype(BF16)

    @pl.loop(0, planes // 2)
    def _(jj):
        j = (spot // 2 + jj) % (planes // 2)
        total = gp_acc[g_tile(j), :] + dot(g_all[last, g_tile(j)], att_last, (0, 0))
        gp_acc[g_tile(j), :] = total
        gp_send[g_tile(j), :] = total.astype(BF16)
        for side in range(2):
            peer = j * 2 + side

            @pl.when(peer != spot)
            def _():
                rs_copy(peer).start()

    gp_sum[...] = gp_acc[two(spot), :]

    @pl.loop(1, planes)
    def _(step):
        peer = (spot + planes - step) % planes
        arrived(gp_recv.at[peer], rs_recv_sem.at[peer])
        gp_sum[...] += gp_recv[peer].astype(F32)

    def own_half(side):
        return pl.ds(pl.multiple_of(side * piece, piece), piece)

    pair_copy = remote(
        gp_sum.at[own_half(1 - z_lo), :], gp_pair, pair_sem.at[0], pair_sem.at[1], dp=pair
    )
    pair_copy.start()
    pair_copy.wait()
    gp_last[...] = (gp_sum[own_half(z_lo), :] + gp_pair[...]).astype(BF16)

    def land_copy(step):
        return remote(
            gp_last,
            land_out.at[cam],
            land_send_sem.at[step],
            land_recv_sem.at[cam],
            cam=(cam + step) % 8,
        )

    pltpu.make_async_copy(gp_last, land_out.at[cam], land_recv_sem.at[cam]).start()

    @pl.loop(1, 8)
    def _(step):
        land_copy(step).start()

    @pl.loop(0, 8)
    def _(source):
        arrived(land_out.at[source], land_recv_sem.at[source])

    for j in range(3):

        @pl.loop(0, 8)
        def _(source):
            arrived(outs[j].at[:, cols(source)], d_recv_sem.at[source, j])

    for j in range(3):
        for slot in range(7):
            qkv_copy(j, others[slot], slot).wait_send()
            d_direct(j, others[slot], slot).wait_send()
    w_copy(pair, w_send_sem.at[0]).wait_send()

    @pl.loop(1, planes)
    def _(step):
        w_copy(in_plane(step) * 2 + z_lo, w_send_sem.at[step]).wait_send()
        w_forward(step).wait_send()
        rs_copy(in_plane(step)).wait_send()

    for part in range(2):
        for slot in range(3):
            g_own(part, slot, g_near[slot]).wait_send()
        for slot in range(4):
            g_pass(cam, part, g_fwd_sem.at[slot, part], sibling).wait_send()

    @pl.loop(1, 8)
    def _(step):
        land_copy(step).wait_send()


def local(grad_out, query_act, key_act, value_act, out_proj, view_counts, view_slots):
    rows, model = grad_out.shape
    devices_dp = lax.axis_size("dp")
    planes = devices_dp // 2
    piece = out_proj.shape[0]
    width = query_act.shape[1] // 8
    tokens = rows * 8
    dims = (planes, rows, width, piece)
    any_spec = pl.BlockSpec(memory_space=pl.ANY)
    dma = pltpu.SemaphoreType.DMA
    gradient = jax.ShapeDtypeStruct(query_act.shape, BF16)
    *gradients, land = pl.pallas_call(
        functools.partial(kernel, dims),
        out_shape=(gradient, gradient, gradient, jax.ShapeDtypeStruct((8, piece, width), BF16)),
        in_specs=[pl.BlockSpec(memory_space=pltpu.SMEM)] * 2
        + [any_spec] * 5,
        out_specs=(any_spec,) * 4,
        scratch_shapes=[
            pltpu.VMEM((tokens, model), BF16),
            pltpu.VMEM((model, width), BF16),
            pltpu.VMEM((3, tokens, width), BF16),
            pltpu.VMEM((HEADS_HERE, tokens, tokens), F32),
            pltpu.VMEM((tokens, width), F32),
            pltpu.VMEM((tokens, width), F32),
            pltpu.VMEM((tokens, width), F32),
            pltpu.VMEM((3, tokens, width), BF16),
            pltpu.VMEM((model, width), F32),
            pltpu.VMEM((model, width), BF16),
            pltpu.VMEM((planes, 2 * piece, width), BF16),
            pltpu.VMEM((2 * piece, width), F32),
            pltpu.VMEM((piece, width), F32),
            pltpu.VMEM((piece, width), BF16),
            pltpu.SMEM((view_slots.shape[1],), jnp.int32),
            pltpu.VMEM((1, tokens), jnp.int32),
            dma((8, 2)),
            dma((3, 2)),
            dma((4, 2)),
            dma((devices_dp,)),
            dma((planes,)),
            dma((planes,)),
            dma((8, 3)),
            dma((7, 3)),
            dma((8, 3)),
            dma((7, 3)),
            dma((planes,)),
            dma((planes,)),
            dma((2,)),
            dma((8,)),
            dma((8,)),
        ],
        compiler_params=pltpu.CompilerParams(
            collective_id=0, has_side_effects=True, vmem_limit_bytes=60 * 1024 * 1024
        ),
        name="group_backward",
    )(view_counts, view_slots, grad_out, query_act, key_act, value_act, out_proj)

    vmem = pl.BlockSpec(memory_space=pltpu.VMEM)
    return pl.pallas_call(
        results,
        out_shape=(gradient, gradient, gradient, jax.ShapeDtypeStruct((piece, width * 8), F32)),
        in_specs=[any_spec] * 3 + [vmem],
        out_specs=(any_spec, any_spec, any_spec, vmem),
        scratch_shapes=[pltpu.VMEM((3, rows, width * 8), BF16), dma((3,)), dma((3,))],
        name="results",
    )(*gradients, land)


def results(dq_in, dk_in, dv_in, land, dq, dk, dv, gp, held, in_sem, out_sem):
    ins, outs = (dq_in, dk_in, dv_in), (dq, dk, dv)
    load = [pltpu.make_async_copy(ins[j], held.at[j], in_sem.at[j]) for j in range(3)]
    store = [pltpu.make_async_copy(held.at[j], outs[j], out_sem.at[j]) for j in range(3)]
    for copy in load:
        copy.start()
    for j in range(3):
        load[j].wait()
        store[j].start()
    width = land.shape[2]
    for source in range(8):
        gp[:, source * width : (source + 1) * width] = land[source].astype(F32)
    for copy in store:
        copy.wait()


def solution(mesh):
    rows = P(("dp", "cam"), None)
    in_specs = (rows, rows, rows, rows, P("dp", None), P("dp", None), P("dp", None))
    out_specs = (rows, rows, rows, P("dp", None))
    return jax.shard_map(local, mesh=mesh, in_specs=in_specs, out_specs=out_specs, check_vma=False)
```

```python
import functools
import math

import jax
import jax.numpy as jnp
from jax import lax
from jax.experimental import pallas as pl
from jax.experimental.pallas import tpu as pltpu
from jax.sharding import PartitionSpec as P

HEAD_DIM = 128
VIEW_TOK = 64
HEADS_HERE = 2
CHIPS = 4
BF16 = jnp.bfloat16
F32 = jnp.float32
MESH = pl.DeviceIdType.MESH


def dot(a, b, contract):
    return lax.dot_general(a, b, ((contract[:1], contract[1:]), ((), ())), preferred_element_type=F32)


def kernel(
    dims,
    counts,
    slots,
    g_in,
    q_in,
    k_in,
    v_in,
    w_in,
    dq_out,
    dk_out,
    dv_out,
    land_out,
    g_chip,
    w_all,
    qkv,
    probs,
    att,
    att_send,
    att_recv,
    go_send,
    go_all,
    dk_acc,
    dv_acc,
    d_send,
    gp_send,
    first_recv,
    second_send,
    second_recv,
    gp_sum,
    line_send,
    line_recv,
    gp_last,
    slot_obj,
    key_obj,
    w_local_sem,
    w_pair_sem,
    w_one_send,
    w_one_recv,
    w_two_send,
    w_two_recv,
    g_local_sem,
    g_sem,
    qkv_recv_sem,
    qkv_send_sem,
    att_send_sem,
    att_recv_sem,
    go_send_sem,
    go_recv_sem,
    d_recv_sem,
    d_send_sem,
    first_send_sem,
    first_recv_sem,
    second_send_sem,
    second_recv_sem,
    line_send_sem,
    line_recv_sem,
    land_send_sem,
    land_recv_sem,
):
    side, rows, width, piece = dims
    chip_rows = 2 * rows
    tokens = 8 * rows
    model = side * side * 2 * piece
    scale = 1.0 / math.sqrt(HEAD_DIM)
    dp = lax.axis_index("dp")
    cam = lax.axis_index("cam")
    spot, z_lo = dp // 2, dp % 2
    y, x = spot // side, spot % side
    pair = spot * 2 + (1 - z_lo)
    chip, core = cam // 2, cam % 2
    sibling = chip * 2 + (1 - core)
    outs = (dq_out, dk_out, dv_out)
    ins = (q_in, k_in, v_in)

    def block(index):
        return pl.ds(pl.multiple_of(index * rows, rows), rows)

    def chip_block(index):
        return pl.ds(pl.multiple_of(index * chip_rows, chip_rows), chip_rows)

    def cols(index):
        return pl.ds(pl.multiple_of(index * width, width), width)

    def half_piece(index):
        return pl.ds(pl.multiple_of(index * piece, piece), piece)

    def remote(src, dst, send, recv, **where):
        return pltpu.make_async_remote_copy(
            src_ref=src, dst_ref=dst, send_sem=send, recv_sem=recv, device_id=where, device_id_type=MESH
        )

    def arrived(ref, sem):
        pltpu.make_async_copy(ref, ref, sem).wait()

    def at_x(c):
        return (y * side + c) * 2 + z_lo

    def at_y(c):
        return (c * side + x) * 2 + z_lo

    def mine(axis):
        return x if axis == "x" else y

    def other(axis, step):
        return (mine(axis) + step) % side

    def peer(axis, c):
        return at_x(c) if axis == "x" else at_y(c)

    gather_axes = (("y", "x"), ("x", "y"))
    reduce_axes = (("x", "y"), ("y", "x"))

    barrier = pltpu.get_barrier_semaphore()

    def greet(**where):
        pl.semaphore_signal(barrier, inc=1, device_id=where, device_id_type=MESH)

    for step in range(1, side):
        greet(dp=peer("x", other("x", step)))
        greet(dp=peer("y", other("y", step)))
    greet(dp=pair)
    for step in range(1, CHIPS):
        greet(dp=pair, cam=(chip + step) % CHIPS * 2 + core)

    @pl.loop(1, 8)
    def _(step):
        greet(cam=(cam + step) % 8)

    def w_local(c):
        return pltpu.make_async_copy(
            w_in.at[:, cols(c * 2 + core)], w_all.at[c, y, x, half_piece(z_lo), :], w_local_sem.at[c]
        )

    for c in range(CHIPS):
        w_local(c).start()

    def g_local():
        return pltpu.make_async_copy(g_in, g_chip.at[block(core), :], g_local_sem)

    g_local().start()
    pl.semaphore_wait(barrier, 2 * (side - 1) + 1 + (CHIPS - 1) + 7)

    def w_pair(z):
        here = w_all.at[:, y, x, half_piece(z), :]
        return remote(here, here, w_pair_sem.at[0], w_pair_sem.at[1], dp=pair)

    def w_one_ref(half, z, c):
        axis = gather_axes[half][0]
        at = (c, x) if axis == "y" else (y, c)
        return w_all.at[2 * half : 2 * half + 2, at[0], at[1], half_piece(z), :]

    def w_one(half, z, step):
        axis = gather_axes[half][0]
        here = w_one_ref(half, z, mine(axis))
        return remote(
            here,
            here,
            w_one_send.at[half, z, step],
            w_one_recv.at[half, z, mine(axis)],
            dp=peer(axis, other(axis, step)),
        )

    def w_two_ref(half, c):
        if gather_axes[half][1] == "x":
            return w_all.at[2 * half : 2 * half + 2, :, c, :, :]
        return w_all.at[2 * half : 2 * half + 2, c, :, :, :]

    def w_two(half, step):
        axis = gather_axes[half][1]
        here = w_two_ref(half, mine(axis))
        return remote(
            here,
            here,
            w_two_send.at[half, step],
            w_two_recv.at[half, mine(axis)],
            dp=peer(axis, other(axis, step)),
        )

    for c in range(CHIPS):
        w_local(c).wait()
    w_pair(z_lo).start()
    for half in range(2):
        for step in range(1, side):
            w_one(half, z_lo, step).start()

    def qkv_copy(j, step):
        target = (cam + step) % 8
        return remote(
            ins[j].at[:, cols(target)],
            qkv.at[j, block(cam), :],
            qkv_send_sem.at[step, j],
            qkv_recv_sem.at[cam, j],
            cam=target,
        )

    for j in range(3):

        @pl.loop(1, 8)
        def _(step):
            qkv_copy(j, step).start()

        pltpu.make_async_copy(
            ins[j].at[:, cols(cam)], qkv.at[j, block(cam), :], qkv_recv_sem.at[cam, j]
        ).start()

    g_copy = remote(g_in, g_chip.at[block(core), :], g_sem.at[0], g_sem.at[1], cam=sibling)
    g_copy.start()

    arrived(w_all.at[:, y, x, half_piece(1 - z_lo), :], w_pair_sem.at[1])
    for half in range(2):
        for step in range(1, side):
            w_one(half, 1 - z_lo, step).start()

    ends = [counts[0, 0]]
    for o in range(1, counts.shape[1]):
        ends.append(ends[-1] + counts[0, o])
    views = slots.shape[1]
    view_obj = [sum((v >= end).astype(jnp.int32) for end in ends) for v in range(views)]

    @pl.loop(0, views)
    def _(s):
        found = jnp.int32(0)
        for v in range(views):
            found = found + jnp.where(slots[0, v] == s, view_obj[v], 0)
        slot_obj[s] = found

    lane_slot = lax.broadcasted_iota(jnp.int32, (1, tokens), 1) // VIEW_TOK
    lane_obj = jnp.zeros((1, tokens), jnp.int32)
    for s in range(views):
        lane_obj = jnp.where(lane_slot == s, slot_obj[s], lane_obj)
    key_obj[...] = lane_obj
    dk_acc[...] = jnp.zeros_like(dk_acc)
    dv_acc[...] = jnp.zeros_like(dv_acc)

    for half in range(2):
        axis = gather_axes[half][0]
        for step in range(1, side):
            for z in range(2):
                c = other(axis, step)
                arrived(w_one_ref(half, z, c), w_one_recv.at[half, z, c])
    for half in range(2):
        for step in range(1, side):
            w_two(half, step).start()

    for j in range(3):

        @pl.loop(0, 8)
        def _(source):
            arrived(qkv.at[j, block(source), :], qkv_recv_sem.at[source, j])

    def att_copy(c):
        return remote(
            att_send.at[chip_block(c), :],
            att_recv.at[:, cols(chip)],
            att_send_sem.at[c],
            att_recv_sem.at[chip],
            cam=c * 2 + core,
        )

    def nth(u, first, second, third, fourth):
        return jnp.where(u == 0, first, jnp.where(u == 1, second, jnp.where(u == 2, third, fourth)))

    @pl.loop(0, CHIPS)
    def _(u):
        c = (chip + nth(u, 2, 1, 3, 0)) % CHIPS

        @pl.loop(0, 2)
        def _(k):
            r = c * 2 + k
            here = block(r)
            row = lax.broadcasted_iota(jnp.int32, (rows, 1), 0)
            row_obj = jnp.where(row < VIEW_TOK, slot_obj[r * 2], slot_obj[r * 2 + 1])
            same = row_obj == key_obj[...]
            for i in range(HEADS_HERE):
                head = slice(i * HEAD_DIM, (i + 1) * HEAD_DIM)
                scores = dot(qkv[0, here, head], qkv[1, :, head], (1, 1)) * scale
                scores = jnp.where(same, scores, -jnp.inf)
                exps = jnp.exp(scores - jnp.max(scores, axis=1, keepdims=True))
                p = exps * (1.0 / jnp.sum(exps, axis=1, keepdims=True))
                probs[i, here, :] = p
                att[here, head] = dot(p.astype(BF16), qkv[2, :, head], (1, 0))

        there = chip_block(c)

        @pl.when(u < CHIPS - 1)
        def _():
            att_send[there, :] = att[there, :].astype(BF16)
            att_copy(c).start()

        @pl.when(u == CHIPS - 1)
        def _():
            att_recv[:, cols(chip)] = att[there, :].astype(BF16)

    for half in range(2):
        axis = gather_axes[half][1]
        for step in range(1, side):
            c = other(axis, step)
            arrived(w_two_ref(half, c), w_two_recv.at[half, c])
    g_local().wait()
    arrived(g_chip.at[block(1 - core), :], g_sem.at[1])

    def go_copy(c):
        return remote(
            go_send.at[c], go_all.at[chip_block(chip), :], go_send_sem.at[c], go_recv_sem.at[chip], cam=c * 2 + core
        )

    @pl.loop(0, CHIPS)
    def _(u):
        c = (chip + nth(u, 2, 1, 3, 0)) % CHIPS
        grad_att = dot(g_chip[...], w_all[c].reshape(model, width), (1, 0)).astype(BF16)

        @pl.when(u < CHIPS - 1)
        def _():
            go_send[c] = grad_att
            go_copy(c).start()

        @pl.when(u == CHIPS - 1)
        def _():
            go_all[chip_block(chip), :] = grad_att

    for step in range(1, CHIPS):
        c = (chip + step) % CHIPS
        arrived(att_recv.at[:, cols(c)], att_recv_sem.at[c])

    def first_copy(half, step):
        axis = reduce_axes[half][0]
        c = other(axis, step)
        src = gp_send.at[2 * half : 2 * half + 2, :, c] if axis == "x" else gp_send.at[2 * half : 2 * half + 2, c]
        return remote(
            src,
            first_recv.at[half, mine(axis)],
            first_send_sem.at[half, step],
            first_recv_sem.at[half, mine(axis)],
            dp=peer(axis, c),
        )

    for half in range(2):
        att_half = att_recv[:, 2 * half * width : 2 * (half + 1) * width]

        @pl.loop(0, side * side // 2)
        def _(j):
            tile = pl.ds(pl.multiple_of(j * 4 * piece, 128), 4 * piece)
            total = dot(g_chip[:, tile], att_half, (0, 0)).astype(BF16)
            for s in range(2):
                for c in range(2):
                    gp_send[2 * half + c, (2 * j + s) // side, (2 * j + s) % side] = total[
                        s * 2 * piece : (s + 1) * 2 * piece, c * width : (c + 1) * width
                    ]

        for step in range(1, side):
            first_copy(half, step).start()

    def d_copy(j, target):
        return remote(
            d_send.at[j, block(target), :],
            outs[j].at[:, cols(cam)],
            d_send_sem.at[target, j],
            d_recv_sem.at[cam, j],
            cam=target,
        )

    def d_local(j):
        return pltpu.make_async_copy(
            d_send.at[j, block(cam), :], outs[j].at[:, cols(cam)], d_recv_sem.at[cam, j]
        )

    @pl.loop(0, CHIPS)
    def _(t):
        c = (chip + nth(t, 0, 3, 1, 2)) % CHIPS
        here = chip_block(c)

        @pl.when(t > 0)
        def _():
            arrived(go_all.at[here, :], go_recv_sem.at[c])

        for i in range(HEADS_HERE):
            head = slice(i * HEAD_DIM, (i + 1) * HEAD_DIM)
            go = go_all[here, head]
            p = probs[i, here, :]
            delta = jnp.sum(go.astype(F32) * att[here, head], axis=1, keepdims=True)
            ds = (p * (dot(go, qkv[2, :, head], (1, 1)) - delta)).astype(BF16)
            d_send[0, here, head] = (dot(ds, qkv[1, :, head], (1, 0)) * scale).astype(BF16)
            dk_acc[:, head] += dot(ds, qkv[0, here, head], (0, 0))
            dv_acc[:, head] += dot(p.astype(BF16), go, (0, 0))

        @pl.when(t == 0)
        def _():
            d_local(0).start()
            d_copy(0, sibling).start()

        @pl.when(t > 0)
        def _():
            d_copy(0, c * 2).start()
            d_copy(0, c * 2 + 1).start()

    d_send[1] = (dk_acc[...] * scale).astype(BF16)
    d_send[2] = dv_acc[...].astype(BF16)
    for j in range(1, 3):

        @pl.loop(1, 8)
        def _(step):
            d_copy(j, (cam + step) % 8).start()

        d_local(j).start()

    def second_copy(half, step):
        axis = reduce_axes[half][1]
        c = other(axis, step)
        return remote(
            second_send.at[half, c],
            second_recv.at[half, mine(axis)],
            second_send_sem.at[half, step],
            second_recv_sem.at[half, mine(axis)],
            dp=peer(axis, c),
        )

    for half in range(2):
        axis, later = reduce_axes[half]
        for step in range(1, side):
            c = other(axis, step)
            arrived(first_recv.at[half, c], first_recv_sem.at[half, c])

        def partial(i):
            own = (slice(2 * half, 2 * half + 2), i, x) if axis == "x" else (slice(2 * half, 2 * half + 2), y, i)
            total = gp_send[own].astype(F32)
            for step in range(1, side):
                total = total + first_recv[half, other(axis, step), :, i].astype(F32)
            return total

        for step in range(1, side):
            i = other(later, step)
            second_send[half, i] = partial(i).astype(BF16)
            second_copy(half, step).start()
        gp_sum[2 * half : 2 * half + 2] = partial(mine(later))

    for half in range(2):
        later = reduce_axes[half][1]
        for step in range(1, side):
            c = other(later, step)
            arrived(second_recv.at[half, c], second_recv_sem.at[half, c])
            gp_sum[2 * half : 2 * half + 2] += second_recv[half, c].astype(F32)

    line_send[...] = gp_sum[...].astype(BF16)
    here_z = chip * 2 + z_lo

    def line_copy(step):
        target = (here_z + step) % 8
        return remote(
            line_send.at[target // 2, half_piece(target % 2), :],
            line_recv.at[here_z],
            line_send_sem.at[step],
            line_recv_sem.at[here_z],
            dp=spot * 2 + target % 2,
            cam=target // 2 * 2 + core,
        )

    @pl.loop(1, 8)
    def _(step):
        line_copy(step).start()

    total = gp_sum[chip, half_piece(z_lo), :]
    for step in range(1, 8):
        source = (here_z + 8 - step) % 8
        arrived(line_recv.at[source], line_recv_sem.at[source])
        total = total + line_recv[source].astype(F32)
    gp_last[...] = total.astype(BF16)

    def land_copy(step):
        return remote(
            gp_last, land_out.at[cam], land_send_sem.at[step], land_recv_sem.at[cam], cam=(cam + step) % 8
        )

    pltpu.make_async_copy(gp_last, land_out.at[cam], land_recv_sem.at[cam]).start()

    @pl.loop(1, 8)
    def _(step):
        land_copy(step).start()

    for j in range(3):

        @pl.loop(0, 8)
        def _(source):
            arrived(outs[j].at[:, cols(source)], d_recv_sem.at[source, j])

    @pl.loop(0, 8)
    def _(source):
        arrived(land_out.at[source], land_recv_sem.at[source])

    w_pair(z_lo).wait_send()
    g_copy.wait_send()
    for half in range(2):
        for step in range(1, side):
            for z in range(2):
                w_one(half, z, step).wait_send()
            w_two(half, step).wait_send()
            first_copy(half, step).wait_send()
            second_copy(half, step).wait_send()
    for step in range(1, CHIPS):
        c = (chip + step) % CHIPS
        att_copy(c).wait_send()
        go_copy(c).wait_send()

    @pl.loop(1, 8)
    def _(step):
        for j in range(3):
            qkv_copy(j, step).wait_send()
            d_copy(j, (cam + step) % 8).wait_send()
        line_copy(step).wait_send()
        land_copy(step).wait_send()


def local(grad_out, query_act, key_act, value_act, out_proj, view_counts, view_slots):
    rows, model = grad_out.shape
    planes = lax.axis_size("dp") // 2
    side = math.isqrt(planes)
    piece = out_proj.shape[0]
    width = query_act.shape[1] // 8
    tokens = rows * 8
    dims = (side, rows, width, piece)
    any_spec = pl.BlockSpec(memory_space=pl.ANY)
    dma = pltpu.SemaphoreType.DMA
    gradient = jax.ShapeDtypeStruct(query_act.shape, BF16)
    *gradients, land = pl.pallas_call(
        functools.partial(kernel, dims),
        out_shape=(gradient, gradient, gradient, jax.ShapeDtypeStruct((8, piece, width), BF16)),
        in_specs=[pl.BlockSpec(memory_space=pltpu.SMEM)] * 2 + [any_spec] * 5,
        out_specs=(any_spec,) * 4,
        scratch_shapes=[
            pltpu.VMEM((2 * rows, model), BF16),
            pltpu.VMEM((CHIPS, side, side, 2 * piece, width), BF16),
            pltpu.VMEM((3, tokens, width), BF16),
            pltpu.VMEM((HEADS_HERE, tokens, tokens), F32),
            pltpu.VMEM((tokens, width), F32),
            pltpu.VMEM((tokens, width), BF16),
            pltpu.VMEM((2 * rows, CHIPS * width), BF16),
            pltpu.VMEM((CHIPS, 2 * rows, width), BF16),
            pltpu.VMEM((tokens, width), BF16),
            pltpu.VMEM((tokens, width), F32),
            pltpu.VMEM((tokens, width), F32),
            pltpu.VMEM((3, tokens, width), BF16),
            pltpu.VMEM((CHIPS, side, side, 2 * piece, width), BF16),
            pltpu.VMEM((2, side, 2, side, 2 * piece, width), BF16),
            pltpu.VMEM((2, side, 2, 2 * piece, width), BF16),
            pltpu.VMEM((2, side, 2, 2 * piece, width), BF16),
            pltpu.VMEM((CHIPS, 2 * piece, width), F32),
            pltpu.VMEM((CHIPS, 2 * piece, width), BF16),
            pltpu.VMEM((8, piece, width), BF16),
            pltpu.VMEM((piece, width), BF16),
            pltpu.SMEM((view_slots.shape[1],), jnp.int32),
            pltpu.VMEM((1, tokens), jnp.int32),
            dma((CHIPS,)),
            dma((2,)),
            dma((2, 2, side)),
            dma((2, 2, side)),
            dma((2, side)),
            dma((2, side)),
            dma,
            dma((2,)),
            dma((8, 3)),
            dma((8, 3)),
            dma((CHIPS,)),
            dma((CHIPS,)),
            dma((CHIPS,)),
            dma((CHIPS,)),
            dma((8, 3)),
            dma((8, 3)),
            dma((2, side)),
            dma((2, side)),
            dma((2, side)),
            dma((2, side)),
            dma((8,)),
            dma((8,)),
            dma((8,)),
            dma((8,)),
        ],
        compiler_params=pltpu.CompilerParams(
            collective_id=0, has_side_effects=True, vmem_limit_bytes=60 * 1024 * 1024
        ),
        name="group_backward",
    )(view_counts, view_slots, grad_out, query_act, key_act, value_act, out_proj)
    vmem = pl.BlockSpec(memory_space=pltpu.VMEM)
    return pl.pallas_call(
        results,
        out_shape=(gradient, gradient, gradient, jax.ShapeDtypeStruct((piece, width * 8), F32)),
        in_specs=[any_spec] * 3 + [vmem],
        out_specs=(any_spec, any_spec, any_spec, vmem),
        scratch_shapes=[pltpu.VMEM((3, rows, width * 8), BF16), dma((3,)), dma((3,))],
        name="results",
    )(*gradients, land)


def results(dq_in, dk_in, dv_in, land, dq, dk, dv, gp, held, in_sem, out_sem):
    ins, outs = (dq_in, dk_in, dv_in), (dq, dk, dv)
    load = [pltpu.make_async_copy(ins[j], held.at[j], in_sem.at[j]) for j in range(3)]
    store = [pltpu.make_async_copy(held.at[j], outs[j], out_sem.at[j]) for j in range(3)]
    for copy in load:
        copy.start()
    for j in range(3):
        load[j].wait()
        store[j].start()
    width = land.shape[2]
    for source in range(8):
        gp[:, source * width : (source + 1) * width] = land[source].astype(F32)
    for copy in store:
        copy.wait()


def solution(mesh):
    rows = P(("dp", "cam"), None)
    in_specs = (rows, rows, rows, rows, P("dp", None), P("dp", None), P("dp", None))
    out_specs = (rows, rows, rows, P("dp", None))
    return jax.shard_map(local, mesh=mesh, in_specs=in_specs, out_specs=out_specs, check_vma=False)
```

```python
import functools
import math

import jax
import jax.numpy as jnp
from jax import lax
from jax.experimental import pallas as pl
from jax.experimental.pallas import tpu as pltpu
from jax.sharding import PartitionSpec as P

HEAD_DIM = 128
VIEW_TOK = 64
HEADS_HERE = 2
CHIPS = 4
BF16 = jnp.bfloat16
F32 = jnp.float32
MESH = pl.DeviceIdType.MESH


def dot(a, b, contract):
    return lax.dot_general(a, b, ((contract[:1], contract[1:]), ((), ())), preferred_element_type=F32)


def kernel(
    dims,
    counts,
    slots,
    g_in,
    q_in,
    k_in,
    v_in,
    w_in,
    dq_out,
    dk_out,
    dv_out,
    land_out,
    g_chip,
    w_all,
    qkv,
    probs,
    att,
    att_send,
    att_recv,
    go_send,
    go_all,
    dk_acc,
    dv_acc,
    d_send,
    gp_send,
    far_recv,
    first_recv,
    second_send,
    second_recv,
    gp_sum,
    line_send,
    line_recv,
    gp_last,
    slot_obj,
    key_obj,
    w_local_sem,
    w_pair_sem,
    w_one_send,
    w_one_recv,
    w_two_send,
    w_pass_send,
    w_two_recv,
    g_local_sem,
    g_sem,
    qkv_recv_sem,
    qkv_send_sem,
    att_send_sem,
    att_recv_sem,
    go_send_sem,
    go_recv_sem,
    d_recv_sem,
    d_send_sem,
    far_send_sem,
    far_recv_sem,
    first_send_sem,
    first_recv_sem,
    second_send_sem,
    second_recv_sem,
    line_send_sem,
    line_recv_sem,
    land_send_sem,
    land_recv_sem,
):
    side, rows, width, piece = dims
    chip_rows = 2 * rows
    tokens = 8 * rows
    model = side * side * 2 * piece
    scale = 1.0 / math.sqrt(HEAD_DIM)
    dp = lax.axis_index("dp")
    cam = lax.axis_index("cam")
    spot, z_lo = dp // 2, dp % 2
    y, x = spot // side, spot % side
    pair = spot * 2 + (1 - z_lo)
    chip, core = cam // 2, cam % 2
    sibling = chip * 2 + (1 - core)
    outs = (dq_out, dk_out, dv_out)
    ins = (q_in, k_in, v_in)

    def block(index):
        return pl.ds(pl.multiple_of(index * rows, rows), rows)

    def chip_block(index):
        return pl.ds(pl.multiple_of(index * chip_rows, chip_rows), chip_rows)

    def cols(index):
        return pl.ds(pl.multiple_of(index * width, width), width)

    def half_piece(index):
        return pl.ds(pl.multiple_of(index * piece, piece), piece)

    def remote(src, dst, send, recv, **where):
        return pltpu.make_async_remote_copy(
            src_ref=src, dst_ref=dst, send_sem=send, recv_sem=recv, device_id=where, device_id_type=MESH
        )

    def arrived(ref, sem):
        pltpu.make_async_copy(ref, ref, sem).wait()

    def at_x(c):
        return (y * side + c) * 2 + z_lo

    def at_y(c):
        return (c * side + x) * 2 + z_lo

    def mine(axis):
        return x if axis == "x" else y

    def other(axis, step):
        return (mine(axis) + step) % side

    def peer(axis, c):
        return at_x(c) if axis == "x" else at_y(c)

    gather_axes = (("y", "x"), ("x", "y"))
    reduce_axes = (("x", "y"), ("y", "x"))

    barrier = pltpu.get_barrier_semaphore()

    def greet(**where):
        pl.semaphore_signal(barrier, inc=1, device_id=where, device_id_type=MESH)

    for step in range(1, side):
        greet(dp=peer("x", other("x", step)))
        greet(dp=peer("y", other("y", step)))
    greet(dp=pair)
    for step in range(1, CHIPS):
        greet(dp=pair, cam=(chip + step) % CHIPS * 2 + core)

    @pl.loop(1, 8)
    def _(step):
        greet(cam=(cam + step) % 8)

    def w_local(c):
        return pltpu.make_async_copy(
            w_in.at[:, cols(c * 2 + core)], w_all.at[c, y, x, half_piece(z_lo), :], w_local_sem.at[c]
        )

    for c in range(CHIPS):
        w_local(c).start()

    def g_local():
        return pltpu.make_async_copy(g_in, g_chip.at[block(core), :], g_local_sem)

    g_local().start()
    pl.semaphore_wait(barrier, 2 * (side - 1) + 1 + (CHIPS - 1) + 7)

    def w_pair_ref(half, z):
        return w_all.at[2 * half : 2 * half + 2, y, x, half_piece(z), :]

    def w_pair(half):
        here = w_pair_ref(half, z_lo)
        there = (chip + half * (CHIPS - 1 + 2 * z_lo)) % CHIPS
        return remote(
            here, here, w_pair_sem.at[0, half], w_pair_sem.at[1, half], dp=pair, cam=there * 2 + core
        )

    def w_one_ref(half, z, c):
        axis = gather_axes[half][0]
        at = (c, x) if axis == "y" else (y, c)
        return w_all.at[2 * half : 2 * half + 2, at[0], at[1], half_piece(z), :]

    def w_one(half, z, step):
        axis = gather_axes[half][0]
        here = w_one_ref(half, z, mine(axis))
        return remote(
            here,
            here,
            w_one_send.at[half, z, step],
            w_one_recv.at[half, z, mine(axis)],
            dp=peer(axis, other(axis, step)),
        )

    def w_two_ref(half, z, c):
        if gather_axes[half][1] == "x":
            return w_all.at[2 * half : 2 * half + 2, :, c, half_piece(z), :]
        return w_all.at[2 * half : 2 * half + 2, c, :, half_piece(z), :]

    def w_two(half, z, way):
        axis = gather_axes[half][1]
        here = w_two_ref(half, z, mine(axis))
        return remote(
            here,
            here,
            w_two_send.at[half, z, way],
            w_two_recv.at[half, z, mine(axis)],
            dp=peer(axis, other(axis, 1 if way == 0 else side - 1)),
        )

    def w_from(half, z):
        return other(gather_axes[half][1], side - 1 + 2 * z)

    def w_pass(half, z):
        axis = gather_axes[half][1]
        here = w_two_ref(half, z, w_from(half, z))
        return remote(
            here,
            here,
            w_pass_send.at[half, z],
            w_two_recv.at[half, z, w_from(half, z)],
            dp=peer(axis, other(axis, side + 1 - 2 * z)),
        )

    def w_two_wait(half, z, c):
        arrived(w_two_ref(half, z, c), w_two_recv.at[half, z, c])

    for c in range(CHIPS):
        w_local(c).wait()
    for half in range(2):
        w_pair(half).start()
    for half in range(2):
        for step in range(1, side):
            w_one(half, z_lo, step).start()

    def qkv_copy(j, step):
        target = (cam + step) % 8
        return remote(
            ins[j].at[:, cols(target)],
            qkv.at[j, block(cam), :],
            qkv_send_sem.at[step, j],
            qkv_recv_sem.at[cam, j],
            cam=target,
        )

    def qkv_start(j):
        @pl.loop(1, 8)
        def _(step):
            qkv_copy(j, step).start()

        pltpu.make_async_copy(
            ins[j].at[:, cols(cam)], qkv.at[j, block(cam), :], qkv_recv_sem.at[cam, j]
        ).start()

    qkv_start(0)

    g_copy = remote(g_in, g_chip.at[block(core), :], g_sem.at[0], g_sem.at[1], cam=sibling)
    g_copy.start()

    for half in range(2):
        arrived(w_pair_ref(half, 1 - z_lo), w_pair_sem.at[1, half])
        for step in range(1, side):
            w_one(half, 1 - z_lo, step).start()
    qkv_start(1)

    ends = [counts[0, 0]]
    for o in range(1, counts.shape[1]):
        ends.append(ends[-1] + counts[0, o])
    views = slots.shape[1]
    view_obj = [sum((v >= end).astype(jnp.int32) for end in ends) for v in range(views)]

    @pl.loop(0, views)
    def _(s):
        found = jnp.int32(0)
        for v in range(views):
            found = found + jnp.where(slots[0, v] == s, view_obj[v], 0)
        slot_obj[s] = found

    lane_slot = lax.broadcasted_iota(jnp.int32, (1, tokens), 1) // VIEW_TOK
    lane_obj = jnp.zeros((1, tokens), jnp.int32)
    for s in range(views):
        lane_obj = jnp.where(lane_slot == s, slot_obj[s], lane_obj)
    key_obj[...] = lane_obj
    dk_acc[...] = jnp.zeros_like(dk_acc)
    dv_acc[...] = jnp.zeros_like(dv_acc)

    for z in (z_lo, 1 - z_lo):
        for half in range(2):
            axis = gather_axes[half][0]
            for step in range(1, side):
                c = other(axis, step)
                arrived(w_one_ref(half, z, c), w_one_recv.at[half, z, c])
            for way in range(2):
                w_two(half, z, way).start()
        if z is z_lo:
            qkv_start(2)
    for j in range(3):

        @pl.loop(0, 8)
        def _(source):
            arrived(qkv.at[j, block(source), :], qkv_recv_sem.at[source, j])

    def att_copy(c):
        return remote(
            att_send.at[chip_block(c), :],
            att_recv.at[:, cols(chip)],
            att_send_sem.at[c],
            att_recv_sem.at[chip],
            cam=c * 2 + core,
        )

    def nth(u, first, second, third, fourth):
        return jnp.where(u == 0, first, jnp.where(u == 1, second, jnp.where(u == 2, third, fourth)))

    @pl.loop(0, CHIPS)
    def _(u):
        c = (chip + nth(u, 2, 1, 3, 0)) % CHIPS

        @pl.loop(0, 2)
        def _(k):
            r = c * 2 + k
            here = block(r)
            row = lax.broadcasted_iota(jnp.int32, (rows, 1), 0)
            row_obj = jnp.where(row < VIEW_TOK, slot_obj[r * 2], slot_obj[r * 2 + 1])
            same = row_obj == key_obj[...]
            for i in range(HEADS_HERE):
                head = slice(i * HEAD_DIM, (i + 1) * HEAD_DIM)
                scores = dot(qkv[0, here, head], qkv[1, :, head], (1, 1)) * scale
                scores = jnp.where(same, scores, -jnp.inf)
                exps = jnp.exp(scores - jnp.max(scores, axis=1, keepdims=True))
                p = exps * (1.0 / jnp.sum(exps, axis=1, keepdims=True))
                probs[i, here, :] = p
                att[here, head] = dot(p.astype(BF16), qkv[2, :, head], (1, 0))

        there = chip_block(c)

        @pl.when(u < 2)
        def _():
            z = jnp.where(u == 0, z_lo, 1 - z_lo)
            for half in range(2):
                w_two_wait(half, z, w_from(half, z))
                w_pass(half, z).start()

        @pl.when(u < CHIPS - 1)
        def _():
            att_send[there, :] = att[there, :].astype(BF16)
            att_copy(c).start()

        @pl.when(u == CHIPS - 1)
        def _():
            att_recv[:, cols(chip)] = att[there, :].astype(BF16)

    g_local().wait()
    arrived(g_chip.at[block(1 - core), :], g_sem.at[1])

    for step in range(1, CHIPS):
        c = (chip + step) % CHIPS
        arrived(att_recv.at[:, cols(c)], att_recv_sem.at[c])

    def first_part(half, part, c):
        if reduce_axes[half][0] == "x":
            return gp_send.at[2 * half + part, :, c]
        return gp_send.at[2 * half + part, c]

    def toward(half, part):
        return other(reduce_axes[half][0], 1 if part == 0 else side - 1)

    def far_copy(half, part):
        axis = reduce_axes[half][0]
        return remote(
            first_part(half, part, other(axis, 2)),
            far_recv.at[half, part],
            far_send_sem.at[half, part],
            far_recv_sem.at[half, part],
            dp=peer(axis, toward(half, part)),
        )

    def first_copy(half, way, part):
        return remote(
            first_part(half, part, toward(half, way)),
            first_recv.at[half, way, part],
            first_send_sem.at[half, way, part],
            first_recv_sem.at[half, way, part],
            dp=peer(reduce_axes[half][0], toward(half, way)),
        )

    for half in range(2):
        att_half = att_recv[:, 2 * half * width : 2 * (half + 1) * width]

        @pl.loop(0, side * side // 2)
        def _(j):
            tile = pl.ds(pl.multiple_of(j * 4 * piece, 128), 4 * piece)
            total = dot(g_chip[:, tile], att_half, (0, 0)).astype(BF16)
            for s in range(2):
                for c in range(2):
                    gp_send[2 * half + c, (2 * j + s) // side, (2 * j + s) % side] = total[
                        s * 2 * piece : (s + 1) * 2 * piece, c * width : (c + 1) * width
                    ]

        for part in range(2):
            far_copy(half, part).start()

    for half in range(2):
        axis = gather_axes[half][1]
        for z in range(2):
            w_two_wait(half, z, other(axis, 1 + (side - 2) * z))
            for step in range(2, side - 1):
                w_two_wait(half, z, other(axis, step))
    def go_copy(c):
        return remote(
            go_send.at[c], go_all.at[chip_block(chip), :], go_send_sem.at[c], go_recv_sem.at[chip], cam=c * 2 + core
        )

    @pl.loop(0, CHIPS)
    def _(u):
        c = (chip + nth(u, 2, 1, 3, 0)) % CHIPS
        grad_att = dot(g_chip[...], w_all[c].reshape(model, width), (1, 0)).astype(BF16)

        @pl.when(u < CHIPS - 1)
        def _():
            go_send[c] = grad_att
            go_copy(c).start()

        @pl.when(u == CHIPS - 1)
        def _():
            go_all[chip_block(chip), :] = grad_att

    for half in range(2):
        for part in range(2):
            first_copy(half, 1 - part, part).start()

    def d_copy(j, target):
        return remote(
            d_send.at[j, block(target), :],
            outs[j].at[:, cols(cam)],
            d_send_sem.at[target, j],
            d_recv_sem.at[cam, j],
            cam=target,
        )

    def d_local(j):
        return pltpu.make_async_copy(
            d_send.at[j, block(cam), :], outs[j].at[:, cols(cam)], d_recv_sem.at[cam, j]
        )

    @pl.loop(0, CHIPS)
    def _(t):
        c = (chip + nth(t, 0, 3, 1, 2)) % CHIPS
        here = chip_block(c)

        @pl.when(t > 0)
        def _():
            arrived(go_all.at[here, :], go_recv_sem.at[c])

        @pl.when(t == 2)
        def _():
            for half in range(2):
                for part in range(2):
                    arrived(far_recv.at[half, part], far_recv_sem.at[half, part])
                    own = first_part(half, part, toward(half, part))
                    own[...] = (own[...].astype(F32) + far_recv[half, part].astype(F32)).astype(BF16)
                    first_copy(half, part, part).start()

        for i in range(HEADS_HERE):
            head = slice(i * HEAD_DIM, (i + 1) * HEAD_DIM)
            go = go_all[here, head]
            p = probs[i, here, :]
            delta = jnp.sum(go.astype(F32) * att[here, head], axis=1, keepdims=True)
            ds = (p * (dot(go, qkv[2, :, head], (1, 1)) - delta)).astype(BF16)
            d_send[0, here, head] = (dot(ds, qkv[1, :, head], (1, 0)) * scale).astype(BF16)
            dk_acc[:, head] += dot(ds, qkv[0, here, head], (0, 0))
            dv_acc[:, head] += dot(p.astype(BF16), go, (0, 0))

        @pl.when(t == 0)
        def _():
            d_local(0).start()
            d_copy(0, sibling).start()

        @pl.when(t > 0)
        def _():
            d_copy(0, c * 2).start()
            d_copy(0, c * 2 + 1).start()

    d_send[1] = (dk_acc[...] * scale).astype(BF16)
    d_send[2] = dv_acc[...].astype(BF16)
    for j in range(1, 3):

        @pl.loop(1, 8)
        def _(step):
            d_copy(j, (cam + step) % 8).start()

        d_local(j).start()

    def second_copy(half, step):
        axis = reduce_axes[half][1]
        c = other(axis, step)
        return remote(
            second_send.at[half, c],
            second_recv.at[half, mine(axis)],
            second_send_sem.at[half, step],
            second_recv_sem.at[half, mine(axis)],
            dp=peer(axis, c),
        )

    for half in range(2):
        axis, later = reduce_axes[half]
        for way in range(2):
            for part in range(2):
                arrived(first_recv.at[half, way, part], first_recv_sem.at[half, way, part])

        def partial(i):
            own = (slice(2 * half, 2 * half + 2), i, x) if axis == "x" else (slice(2 * half, 2 * half + 2), y, i)
            total = gp_send[own].astype(F32)
            for way in range(2):
                total = total + first_recv[half, way, :, i].astype(F32)
            return total

        for step in range(1, side):
            i = other(later, step)
            second_send[half, i] = partial(i).astype(BF16)
            second_copy(half, step).start()
        gp_sum[2 * half : 2 * half + 2] = partial(mine(later))

    for half in range(2):
        later = reduce_axes[half][1]
        for step in range(1, side):
            c = other(later, step)
            arrived(second_recv.at[half, c], second_recv_sem.at[half, c])
            gp_sum[2 * half : 2 * half + 2] += second_recv[half, c].astype(F32)

    line_send[...] = gp_sum[...].astype(BF16)
    here_z = chip * 2 + z_lo

    def line_copy(step):
        target = (here_z + step) % 8
        return remote(
            line_send.at[target // 2, half_piece(target % 2), :],
            line_recv.at[here_z],
            line_send_sem.at[step],
            line_recv_sem.at[here_z],
            dp=spot * 2 + target % 2,
            cam=target // 2 * 2 + core,
        )

    @pl.loop(1, 8)
    def _(step):
        line_copy(step).start()

    total = gp_sum[chip, half_piece(z_lo), :]
    for step in range(1, 8):
        source = (here_z + 8 - step) % 8
        arrived(line_recv.at[source], line_recv_sem.at[source])
        total = total + line_recv[source].astype(F32)
    gp_last[...] = total.astype(BF16)

    def land_copy(step):
        target = (chip + step) % CHIPS * 2 + core if step else sibling
        return remote(gp_last, land_out.at[cam], land_send_sem.at[step], land_recv_sem.at[cam], cam=target)

    def land_pass(step):
        source = (chip + step) % CHIPS * 2 + core
        here = land_out.at[source]
        return remote(here, here, land_send_sem.at[CHIPS + step], land_recv_sem.at[source], cam=sibling)

    for step in (2, 1, 3, 0):
        land_copy(step).start()
    pltpu.make_async_copy(gp_last, land_out.at[cam], land_recv_sem.at[cam]).start()
    for step in (1, 3, 2):
        source = (chip + step) % CHIPS * 2 + core
        arrived(land_out.at[source], land_recv_sem.at[source])
        land_pass(step).start()

    for j in range(3):

        @pl.loop(0, 8)
        def _(source):
            arrived(outs[j].at[:, cols(source)], d_recv_sem.at[source, j])

    arrived(land_out.at[cam], land_recv_sem.at[cam])
    for step in range(CHIPS):
        source = (chip + step) % CHIPS * 2 + 1 - core
        arrived(land_out.at[source], land_recv_sem.at[source])

    for half in range(2):
        w_pair(half).wait_send()
    g_copy.wait_send()
    for half in range(2):
        for step in range(1, side):
            for z in range(2):
                w_one(half, z, step).wait_send()
            second_copy(half, step).wait_send()
        for z in range(2):
            w_pass(half, z).wait_send()
            far_copy(half, z).wait_send()
            for part in range(2):
                first_copy(half, z, part).wait_send()
            for way in range(2):
                w_two(half, z, way).wait_send()
    for step in range(1, CHIPS):
        c = (chip + step) % CHIPS
        att_copy(c).wait_send()
        go_copy(c).wait_send()

    @pl.loop(1, 8)
    def _(step):
        for j in range(3):
            qkv_copy(j, step).wait_send()
            d_copy(j, (cam + step) % 8).wait_send()
        line_copy(step).wait_send()

    for step in range(CHIPS):
        land_copy(step).wait_send()
        if step:
            land_pass(step).wait_send()


def local(grad_out, query_act, key_act, value_act, out_proj, view_counts, view_slots):
    rows, model = grad_out.shape
    planes = lax.axis_size("dp") // 2
    side = math.isqrt(planes)
    piece = out_proj.shape[0]
    width = query_act.shape[1] // 8
    tokens = rows * 8
    dims = (side, rows, width, piece)
    any_spec = pl.BlockSpec(memory_space=pl.ANY)
    dma = pltpu.SemaphoreType.DMA
    gradient = jax.ShapeDtypeStruct(query_act.shape, BF16)
    *gradients, land = pl.pallas_call(
        functools.partial(kernel, dims),
        out_shape=(gradient, gradient, gradient, jax.ShapeDtypeStruct((8, piece, width), BF16)),
        in_specs=[pl.BlockSpec(memory_space=pltpu.SMEM)] * 2 + [any_spec] * 5,
        out_specs=(any_spec,) * 4,
        scratch_shapes=[
            pltpu.VMEM((2 * rows, model), BF16),
            pltpu.VMEM((CHIPS, side, side, 2 * piece, width), BF16),
            pltpu.VMEM((3, tokens, width), BF16),
            pltpu.VMEM((HEADS_HERE, tokens, tokens), F32),
            pltpu.VMEM((tokens, width), F32),
            pltpu.VMEM((tokens, width), BF16),
            pltpu.VMEM((2 * rows, CHIPS * width), BF16),
            pltpu.VMEM((CHIPS, 2 * rows, width), BF16),
            pltpu.VMEM((tokens, width), BF16),
            pltpu.VMEM((tokens, width), F32),
            pltpu.VMEM((tokens, width), F32),
            pltpu.VMEM((3, tokens, width), BF16),
            pltpu.VMEM((CHIPS, side, side, 2 * piece, width), BF16),
            pltpu.VMEM((2, 2, side, 2 * piece, width), BF16),
            pltpu.VMEM((2, 2, 2, side, 2 * piece, width), BF16),
            pltpu.VMEM((2, side, 2, 2 * piece, width), BF16),
            pltpu.VMEM((2, side, 2, 2 * piece, width), BF16),
            pltpu.VMEM((CHIPS, 2 * piece, width), F32),
            pltpu.VMEM((CHIPS, 2 * piece, width), BF16),
            pltpu.VMEM((8, piece, width), BF16),
            pltpu.VMEM((piece, width), BF16),
            pltpu.SMEM((view_slots.shape[1],), jnp.int32),
            pltpu.VMEM((1, tokens), jnp.int32),
            dma((CHIPS,)),
            dma((2, 2)),
            dma((2, 2, side)),
            dma((2, 2, side)),
            dma((2, 2, 2)),
            dma((2, 2)),
            dma((2, 2, side)),
            dma,
            dma((2,)),
            dma((8, 3)),
            dma((8, 3)),
            dma((CHIPS,)),
            dma((CHIPS,)),
            dma((CHIPS,)),
            dma((CHIPS,)),
            dma((8, 3)),
            dma((8, 3)),
            dma((2, 2)),
            dma((2, 2)),
            dma((2, 2, 2)),
            dma((2, 2, 2)),
            dma((2, side)),
            dma((2, side)),
            dma((8,)),
            dma((8,)),
            dma((8,)),
            dma((8,)),
        ],
        compiler_params=pltpu.CompilerParams(
            collective_id=0, has_side_effects=True, vmem_limit_bytes=60 * 1024 * 1024
        ),
        name="group_backward",
    )(view_counts, view_slots, grad_out, query_act, key_act, value_act, out_proj)
    return pl.pallas_call(
        results,
        out_shape=(gradient, gradient, gradient, jax.ShapeDtypeStruct((piece, width * 8), F32)),
        in_specs=[any_spec] * 4,
        out_specs=(any_spec,) * 4,
        scratch_shapes=[
            pltpu.VMEM((3, rows, width * 8), BF16),
            pltpu.VMEM((8, piece, width), BF16),
            pltpu.VMEM((piece, width * 8), F32),
            dma((7,)),
            dma((7,)),
        ],
        name="results",
    )(*gradients, land)


def results(dq_in, dk_in, dv_in, land_in, dq, dk, dv, gp, held, land, wide, in_sem, out_sem):
    half = dq.shape[0] // 2
    load = [pltpu.make_async_copy(land_in, land, in_sem.at[6])]
    store = [pltpu.make_async_copy(wide, gp, out_sem.at[6])]
    for j, (a, b) in enumerate(((dq_in, dq), (dk_in, dk), (dv_in, dv))):
        for k in range(2):
            part = pl.ds(k * half, half)
            load.append(pltpu.make_async_copy(a.at[part], held.at[j, part], in_sem.at[2 * j + k]))
            store.append(pltpu.make_async_copy(held.at[j, part], b.at[part], out_sem.at[2 * j + k]))
    for copy in load:
        copy.start()
    width = land.shape[2]
    for index in (*range(1, 7), 0):
        load[index].wait()
        if index == 0:
            for source in range(8):
                wide[:, source * width : (source + 1) * width] = land[source].astype(F32)
        store[index].start()
    for copy in store:
        copy.wait()


def solution(mesh):
    rows = P(("dp", "cam"), None)
    in_specs = (rows, rows, rows, rows, P("dp", None), P("dp", None), P("dp", None))
    out_specs = (rows, rows, rows, P("dp", None))
    return jax.shard_map(local, mesh=mesh, in_specs=in_specs, out_specs=out_specs, check_vma=False)
```

```python
import functools
import math

import jax
import jax.numpy as jnp
from jax import lax
from jax.experimental import pallas as pl
from jax.experimental.pallas import tpu as pltpu
from jax.sharding import PartitionSpec as P

HEAD_DIM = 128
VIEW_TOK = 64
HEADS_HERE = 2
CHIPS = 4
BF16 = jnp.bfloat16
F32 = jnp.float32
MESH = pl.DeviceIdType.MESH


def dot(a, b, contract):
    return lax.dot_general(a, b, ((contract[:1], contract[1:]), ((), ())), preferred_element_type=F32)


def kernel(
    dims,
    counts,
    slots,
    g_in,
    q_in,
    k_in,
    v_in,
    w_in,
    dq_out,
    dk_out,
    dv_out,
    land_out,
    g_chip,
    w_all,
    qkv,
    probs,
    att,
    att_send,
    att_recv,
    go_send,
    go_all,
    dk_acc,
    dv_acc,
    d_send,
    gp_send,
    far_recv,
    first_recv,
    second_send,
    second_recv,
    gp_sum,
    line_send,
    line_recv,
    gp_last,
    slot_obj,
    key_obj,
    w_local_sem,
    w_pair_sem,
    w_one_send,
    w_one_recv,
    w_two_send,
    w_pass_send,
    w_two_recv,
    g_local_sem,
    g_sem,
    qkv_recv_sem,
    qkv_send_sem,
    att_send_sem,
    att_recv_sem,
    go_send_sem,
    go_recv_sem,
    d_recv_sem,
    d_send_sem,
    far_send_sem,
    far_recv_sem,
    first_send_sem,
    first_recv_sem,
    second_send_sem,
    second_recv_sem,
    line_send_sem,
    line_recv_sem,
    land_send_sem,
    land_recv_sem,
):
    side, rows, width, piece = dims
    chip_rows = 2 * rows
    tokens = 8 * rows
    model = side * side * 2 * piece
    scale = 1.0 / math.sqrt(HEAD_DIM)
    dp = lax.axis_index("dp")
    cam = lax.axis_index("cam")
    spot, z_lo = dp // 2, dp % 2
    y, x = spot // side, spot % side
    pair = spot * 2 + (1 - z_lo)
    chip, core = cam // 2, cam % 2
    sibling = chip * 2 + (1 - core)
    outs = (dq_out, dk_out, dv_out)
    ins = (q_in, k_in, v_in)

    def block(index):
        return pl.ds(pl.multiple_of(index * rows, rows), rows)

    def chip_block(index):
        return pl.ds(pl.multiple_of(index * chip_rows, chip_rows), chip_rows)

    def cols(index):
        return pl.ds(pl.multiple_of(index * width, width), width)

    def head_cols(index, i):
        return pl.ds(pl.multiple_of(index * width + i * HEAD_DIM, HEAD_DIM), HEAD_DIM)

    def half_piece(index):
        return pl.ds(pl.multiple_of(index * piece, piece), piece)

    def remote(src, dst, send, recv, **where):
        return pltpu.make_async_remote_copy(
            src_ref=src, dst_ref=dst, send_sem=send, recv_sem=recv, device_id=where, device_id_type=MESH
        )

    def arrived(ref, sem):
        pltpu.make_async_copy(ref, ref, sem).wait()

    def at_x(c):
        return (y * side + c) * 2 + z_lo

    def at_y(c):
        return (c * side + x) * 2 + z_lo

    def mine(axis):
        return x if axis == "x" else y

    def other(axis, step):
        return (mine(axis) + step) % side

    def peer(axis, c):
        return at_x(c) if axis == "x" else at_y(c)

    gather_axes = (("y", "x"), ("x", "y"))
    reduce_axes = (("x", "y"), ("y", "x"))

    barrier = pltpu.get_barrier_semaphore()

    def greet(**where):
        pl.semaphore_signal(barrier, inc=1, device_id=where, device_id_type=MESH)

    for step in range(1, side):
        greet(dp=peer("x", other("x", step)))
        greet(dp=peer("y", other("y", step)))
    greet(dp=pair)
    for step in range(1, CHIPS):
        greet(dp=pair, cam=(chip + step) % CHIPS * 2 + core)

    @pl.loop(1, 8)
    def _(step):
        greet(cam=(cam + step) % 8)

    def w_local(c):
        return pltpu.make_async_copy(
            w_in.at[:, cols(c * 2 + core)], w_all.at[c, y, x, half_piece(z_lo), :], w_local_sem.at[c]
        )

    for c in range(CHIPS):
        w_local(c).start()

    def g_local():
        return pltpu.make_async_copy(g_in, g_chip.at[block(core), :], g_local_sem)

    g_local().start()
    pl.semaphore_wait(barrier, 2 * (side - 1) + 1 + (CHIPS - 1) + 7)

    def w_pair_ref(half, z):
        return w_all.at[2 * half : 2 * half + 2, y, x, half_piece(z), :]

    def w_pair(half):
        here = w_pair_ref(half, z_lo)
        there = (chip + half * (CHIPS - 1 + 2 * z_lo)) % CHIPS
        return remote(
            here, here, w_pair_sem.at[0, half], w_pair_sem.at[1, half], dp=pair, cam=there * 2 + core
        )

    def w_one_ref(half, z, c):
        axis = gather_axes[half][0]
        at = (c, x) if axis == "y" else (y, c)
        return w_all.at[2 * half : 2 * half + 2, at[0], at[1], half_piece(z), :]

    def w_one(half, z, step):
        axis = gather_axes[half][0]
        here = w_one_ref(half, z, mine(axis))
        return remote(
            here,
            here,
            w_one_send.at[half, z, step],
            w_one_recv.at[half, z, mine(axis)],
            dp=peer(axis, other(axis, step)),
        )

    def w_two_ref(half, z, c):
        if gather_axes[half][1] == "x":
            return w_all.at[2 * half : 2 * half + 2, :, c, half_piece(z), :]
        return w_all.at[2 * half : 2 * half + 2, c, :, half_piece(z), :]

    def w_two(half, z, way):
        axis = gather_axes[half][1]
        here = w_two_ref(half, z, mine(axis))
        return remote(
            here,
            here,
            w_two_send.at[half, z, way],
            w_two_recv.at[half, z, mine(axis)],
            dp=peer(axis, other(axis, 1 if way == 0 else side - 1)),
        )

    def w_from(half, z):
        return other(gather_axes[half][1], side - 1 + 2 * z)

    def w_pass(half, z):
        axis = gather_axes[half][1]
        here = w_two_ref(half, z, w_from(half, z))
        return remote(
            here,
            here,
            w_pass_send.at[half, z],
            w_two_recv.at[half, z, w_from(half, z)],
            dp=peer(axis, other(axis, side + 1 - 2 * z)),
        )

    def w_two_wait(half, z, c):
        arrived(w_two_ref(half, z, c), w_two_recv.at[half, z, c])

    for c in range(CHIPS):
        w_local(c).wait()
    for half in range(2):
        w_pair(half).start()
    for half in range(2):
        for step in range(1, side):
            w_one(half, z_lo, step).start()

    def qkv_copy(j, step):
        target = (cam + step) % 8
        return remote(
            ins[j].at[:, cols(target)],
            qkv.at[j, block(cam), :],
            qkv_send_sem.at[step, j],
            qkv_recv_sem.at[cam, j],
            cam=target,
        )

    def qkv_start(j):
        @pl.loop(1, 8)
        def _(step):
            qkv_copy(j, step).start()

        pltpu.make_async_copy(
            ins[j].at[:, cols(cam)], qkv.at[j, block(cam), :], qkv_recv_sem.at[cam, j]
        ).start()

    qkv_start(0)

    g_copy = remote(g_in, g_chip.at[block(core), :], g_sem.at[0], g_sem.at[1], cam=sibling)
    g_copy.start()

    for half in range(2):
        arrived(w_pair_ref(half, 1 - z_lo), w_pair_sem.at[1, half])
        for step in range(1, side):
            w_one(half, 1 - z_lo, step).start()
    qkv_start(1)

    ends = [counts[0, 0]]
    for o in range(1, counts.shape[1]):
        ends.append(ends[-1] + counts[0, o])
    views = slots.shape[1]
    view_obj = [sum((v >= end).astype(jnp.int32) for end in ends) for v in range(views)]

    @pl.loop(0, views)
    def _(s):
        found = jnp.int32(0)
        for v in range(views):
            found = found + jnp.where(slots[0, v] == s, view_obj[v], 0)
        slot_obj[s] = found

    lane_slot = lax.broadcasted_iota(jnp.int32, (1, tokens), 1) // VIEW_TOK
    lane_obj = jnp.zeros((1, tokens), jnp.int32)
    for s in range(views):
        lane_obj = jnp.where(lane_slot == s, slot_obj[s], lane_obj)
    key_obj[...] = lane_obj
    dk_acc[...] = jnp.zeros_like(dk_acc)
    dv_acc[...] = jnp.zeros_like(dv_acc)

    for z in (z_lo, 1 - z_lo):
        for half in range(2):
            axis = gather_axes[half][0]
            for step in range(1, side):
                c = other(axis, step)
                arrived(w_one_ref(half, z, c), w_one_recv.at[half, z, c])
            for way in range(2):
                w_two(half, z, way).start()
        if z is z_lo:
            qkv_start(2)
    for j in range(3):

        @pl.loop(0, 8)
        def _(source):
            arrived(qkv.at[j, block(source), :], qkv_recv_sem.at[source, j])

    def att_copy(c):
        return remote(
            att_send.at[chip_block(c), :],
            att_recv.at[:, cols(chip)],
            att_send_sem.at[c],
            att_recv_sem.at[chip],
            cam=c * 2 + core,
        )

    def nth(u, first, second, third, fourth):
        return jnp.where(u == 0, first, jnp.where(u == 1, second, jnp.where(u == 2, third, fourth)))

    @pl.loop(0, CHIPS)
    def _(u):
        c = (chip + nth(u, 2, 1, 3, 0)) % CHIPS

        @pl.loop(0, 2)
        def _(k):
            r = c * 2 + k
            here = block(r)
            row = lax.broadcasted_iota(jnp.int32, (rows, 1), 0)
            row_obj = jnp.where(row < VIEW_TOK, slot_obj[r * 2], slot_obj[r * 2 + 1])
            same = row_obj == key_obj[...]
            for i in range(HEADS_HERE):
                head = slice(i * HEAD_DIM, (i + 1) * HEAD_DIM)
                scores = dot(qkv[0, here, head], qkv[1, :, head], (1, 1)) * scale
                scores = jnp.where(same, scores, -jnp.inf)
                exps = jnp.exp(scores - jnp.max(scores, axis=1, keepdims=True))
                p = exps * (1.0 / jnp.sum(exps, axis=1, keepdims=True))
                probs[i, here, :] = p
                att[here, head] = dot(p.astype(BF16), qkv[2, :, head], (1, 0))

        there = chip_block(c)

        @pl.when(u < 2)
        def _():
            z = jnp.where(u == 0, z_lo, 1 - z_lo)
            for half in range(2):
                w_two_wait(half, z, w_from(half, z))
                w_pass(half, z).start()

        @pl.when(u < CHIPS - 1)
        def _():
            att_send[there, :] = att[there, :].astype(BF16)
            att_copy(c).start()

        @pl.when(u == CHIPS - 1)
        def _():
            att_recv[:, cols(chip)] = att[there, :].astype(BF16)

    g_local().wait()
    arrived(g_chip.at[block(1 - core), :], g_sem.at[1])

    for half in range(2):
        axis = gather_axes[half][1]
        for z in range(2):
            w_two_wait(half, z, other(axis, 1 + (side - 2) * z))
            for step in range(2, side - 1):
                w_two_wait(half, z, other(axis, step))
    def go_copy(c):
        return remote(
            go_send.at[c], go_all.at[chip_block(chip), :], go_send_sem.at[c], go_recv_sem.at[chip], cam=c * 2 + core
        )

    @pl.loop(0, CHIPS)
    def _(u):
        c = (chip + nth(u, 2, 1, 3, 0)) % CHIPS
        grad_att = dot(g_chip[...], w_all[c].reshape(model, width), (1, 0)).astype(BF16)

        @pl.when(u < CHIPS - 1)
        def _():
            go_send[c] = grad_att
            go_copy(c).start()

        @pl.when(u == CHIPS - 1)
        def _():
            go_all[chip_block(chip), :] = grad_att

    for step in range(1, CHIPS):
        c = (chip + step) % CHIPS
        arrived(att_recv.at[:, cols(c)], att_recv_sem.at[c])

    def first_part(half, part, c):
        if reduce_axes[half][0] == "x":
            return gp_send.at[2 * half + part, :, c]
        return gp_send.at[2 * half + part, c]

    def toward(half, part):
        return other(reduce_axes[half][0], 1 if part == 0 else side - 1)

    def far_copy(half, part):
        axis = reduce_axes[half][0]
        return remote(
            first_part(half, part, other(axis, 2)),
            far_recv.at[half, part],
            far_send_sem.at[half, part],
            far_recv_sem.at[half, part],
            dp=peer(axis, toward(half, part)),
        )

    def first_copy(half, way, part):
        return remote(
            first_part(half, part, toward(half, way)),
            first_recv.at[half, way, part],
            first_send_sem.at[half, way, part],
            first_recv_sem.at[half, way, part],
            dp=peer(reduce_axes[half][0], toward(half, way)),
        )

    for half in range(2):
        att_half = att_recv[:, 2 * half * width : 2 * (half + 1) * width]

        @pl.loop(0, side * side // 2)
        def _(j):
            tile = pl.ds(pl.multiple_of(j * 4 * piece, 128), 4 * piece)
            total = dot(g_chip[:, tile], att_half, (0, 0)).astype(BF16)
            for s in range(2):
                for c in range(2):
                    gp_send[2 * half + c, (2 * j + s) // side, (2 * j + s) % side] = total[
                        s * 2 * piece : (s + 1) * 2 * piece, c * width : (c + 1) * width
                    ]

        for part in range(2):
            far_copy(half, part).start()

    for half in range(2):
        for part in range(2):
            first_copy(half, 1 - part, part).start()

    def d_copy(j, i, target):
        return remote(
            d_send.at[j, block(target), i * HEAD_DIM : (i + 1) * HEAD_DIM],
            outs[j].at[:, head_cols(cam, i)],
            d_send_sem.at[target, j, i],
            d_recv_sem.at[cam, j, i],
            cam=target,
        )

    def d_local(j, i):
        return pltpu.make_async_copy(
            d_send.at[j, block(cam), i * HEAD_DIM : (i + 1) * HEAD_DIM],
            outs[j].at[:, head_cols(cam, i)],
            d_recv_sem.at[cam, j, i],
        )

    def backward(c, i):
        here = chip_block(c)
        head = slice(i * HEAD_DIM, (i + 1) * HEAD_DIM)
        go = go_all[here, head]
        p = probs[i, here, :]
        delta = jnp.sum(go.astype(F32) * att[here, head], axis=1, keepdims=True)
        ds = (p * (dot(go, qkv[2, :, head], (1, 1)) - delta)).astype(BF16)
        d_send[0, here, head] = (dot(ds, qkv[1, :, head], (1, 0)) * scale).astype(BF16)
        dk_acc[:, head] += dot(ds, qkv[0, here, head], (0, 0))
        dv_acc[:, head] += dot(p.astype(BF16), go, (0, 0))

    for i in range(HEADS_HERE):
        backward(chip, i)
        d_local(0, i).start()
        d_copy(0, i, sibling).start()

    for i in range(HEADS_HERE):
        head = slice(i * HEAD_DIM, (i + 1) * HEAD_DIM)

        @pl.loop(1, CHIPS)
        def _(t):
            c = (chip + nth(t, 0, 3, 1, 2)) % CHIPS
            if i == 0:
                arrived(go_all.at[chip_block(c), :], go_recv_sem.at[c])

                @pl.when(t == 2)
                def _():
                    for half in range(2):
                        for part in range(2):
                            arrived(far_recv.at[half, part], far_recv_sem.at[half, part])
                            own = first_part(half, part, toward(half, part))
                            own[...] = (own[...].astype(F32) + far_recv[half, part].astype(F32)).astype(BF16)
                            first_copy(half, part, part).start()

            backward(c, i)
            d_copy(0, i, c * 2).start()
            d_copy(0, i, c * 2 + 1).start()

        d_send[1, :, head] = (dk_acc[:, head] * scale).astype(BF16)
        d_send[2, :, head] = dv_acc[:, head].astype(BF16)
        for j in range(1, 3):

            @pl.loop(1, 8)
            def _(step):
                d_copy(j, i, (cam + step) % 8).start()

            d_local(j, i).start()

    def second_copy(half, step):
        axis = reduce_axes[half][1]
        c = other(axis, step)
        return remote(
            second_send.at[half, c],
            second_recv.at[half, mine(axis)],
            second_send_sem.at[half, step],
            second_recv_sem.at[half, mine(axis)],
            dp=peer(axis, c),
        )

    for half in range(2):
        axis, later = reduce_axes[half]
        for way in range(2):
            for part in range(2):
                arrived(first_recv.at[half, way, part], first_recv_sem.at[half, way, part])

        def partial(i):
            own = (slice(2 * half, 2 * half + 2), i, x) if axis == "x" else (slice(2 * half, 2 * half + 2), y, i)
            total = gp_send[own].astype(F32)
            for way in range(2):
                total = total + first_recv[half, way, :, i].astype(F32)
            return total

        for step in range(1, side):
            i = other(later, step)
            second_send[half, i] = partial(i).astype(BF16)
            second_copy(half, step).start()
        gp_sum[2 * half : 2 * half + 2] = partial(mine(later))

    for half in range(2):
        later = reduce_axes[half][1]
        for step in range(1, side):
            c = other(later, step)
            arrived(second_recv.at[half, c], second_recv_sem.at[half, c])
            gp_sum[2 * half : 2 * half + 2] += second_recv[half, c].astype(F32)

    line_send[...] = gp_sum[...].astype(BF16)
    here_z = chip * 2 + z_lo

    def line_copy(step):
        target = (here_z + step) % 8
        return remote(
            line_send.at[target // 2, half_piece(target % 2), :],
            line_recv.at[here_z],
            line_send_sem.at[step],
            line_recv_sem.at[here_z],
            dp=spot * 2 + target % 2,
            cam=target // 2 * 2 + core,
        )

    @pl.loop(1, 8)
    def _(step):
        line_copy(step).start()

    total = gp_sum[chip, half_piece(z_lo), :]
    for step in range(1, 8):
        source = (here_z + 8 - step) % 8
        arrived(line_recv.at[source], line_recv_sem.at[source])
        total = total + line_recv[source].astype(F32)
    gp_last[...] = total.astype(BF16)

    def land_copy(step):
        target = (chip + step) % CHIPS * 2 + core if step else sibling
        return remote(gp_last, land_out.at[cam], land_send_sem.at[step], land_recv_sem.at[cam], cam=target)

    def land_pass(step):
        source = (chip + step) % CHIPS * 2 + core
        here = land_out.at[source]
        return remote(here, here, land_send_sem.at[CHIPS + step], land_recv_sem.at[source], cam=sibling)

    for step in (2, 1, 3, 0):
        land_copy(step).start()
    pltpu.make_async_copy(gp_last, land_out.at[cam], land_recv_sem.at[cam]).start()
    for step in (1, 3, 2):
        source = (chip + step) % CHIPS * 2 + core
        arrived(land_out.at[source], land_recv_sem.at[source])
        land_pass(step).start()

    for j in range(3):

        @pl.loop(0, 8)
        def _(source):
            for i in range(HEADS_HERE):
                arrived(outs[j].at[:, head_cols(source, i)], d_recv_sem.at[source, j, i])

    arrived(land_out.at[cam], land_recv_sem.at[cam])
    for step in range(CHIPS):
        source = (chip + step) % CHIPS * 2 + 1 - core
        arrived(land_out.at[source], land_recv_sem.at[source])

    for half in range(2):
        w_pair(half).wait_send()
    g_copy.wait_send()
    for half in range(2):
        for step in range(1, side):
            for z in range(2):
                w_one(half, z, step).wait_send()
            second_copy(half, step).wait_send()
        for z in range(2):
            w_pass(half, z).wait_send()
            far_copy(half, z).wait_send()
            for part in range(2):
                first_copy(half, z, part).wait_send()
            for way in range(2):
                w_two(half, z, way).wait_send()
    for step in range(1, CHIPS):
        c = (chip + step) % CHIPS
        att_copy(c).wait_send()
        go_copy(c).wait_send()

    @pl.loop(1, 8)
    def _(step):
        for j in range(3):
            qkv_copy(j, step).wait_send()
            for i in range(HEADS_HERE):
                d_copy(j, i, (cam + step) % 8).wait_send()
        line_copy(step).wait_send()

    for step in range(CHIPS):
        land_copy(step).wait_send()
        if step:
            land_pass(step).wait_send()


def local(grad_out, query_act, key_act, value_act, out_proj, view_counts, view_slots):
    rows, model = grad_out.shape
    planes = lax.axis_size("dp") // 2
    side = math.isqrt(planes)
    piece = out_proj.shape[0]
    width = query_act.shape[1] // 8
    tokens = rows * 8
    dims = (side, rows, width, piece)
    any_spec = pl.BlockSpec(memory_space=pl.ANY)
    dma = pltpu.SemaphoreType.DMA
    gradient = jax.ShapeDtypeStruct(query_act.shape, BF16)
    *gradients, land = pl.pallas_call(
        functools.partial(kernel, dims),
        out_shape=(gradient, gradient, gradient, jax.ShapeDtypeStruct((8, piece, width), BF16)),
        in_specs=[pl.BlockSpec(memory_space=pltpu.SMEM)] * 2 + [any_spec] * 5,
        out_specs=(any_spec,) * 4,
        scratch_shapes=[
            pltpu.VMEM((2 * rows, model), BF16),
            pltpu.VMEM((CHIPS, side, side, 2 * piece, width), BF16),
            pltpu.VMEM((3, tokens, width), BF16),
            pltpu.VMEM((HEADS_HERE, tokens, tokens), F32),
            pltpu.VMEM((tokens, width), F32),
            pltpu.VMEM((tokens, width), BF16),
            pltpu.VMEM((2 * rows, CHIPS * width), BF16),
            pltpu.VMEM((CHIPS, 2 * rows, width), BF16),
            pltpu.VMEM((tokens, width), BF16),
            pltpu.VMEM((tokens, width), F32),
            pltpu.VMEM((tokens, width), F32),
            pltpu.VMEM((3, tokens, width), BF16),
            pltpu.VMEM((CHIPS, side, side, 2 * piece, width), BF16),
            pltpu.VMEM((2, 2, side, 2 * piece, width), BF16),
            pltpu.VMEM((2, 2, 2, side, 2 * piece, width), BF16),
            pltpu.VMEM((2, side, 2, 2 * piece, width), BF16),
            pltpu.VMEM((2, side, 2, 2 * piece, width), BF16),
            pltpu.VMEM((CHIPS, 2 * piece, width), F32),
            pltpu.VMEM((CHIPS, 2 * piece, width), BF16),
            pltpu.VMEM((8, piece, width), BF16),
            pltpu.VMEM((piece, width), BF16),
            pltpu.SMEM((view_slots.shape[1],), jnp.int32),
            pltpu.VMEM((1, tokens), jnp.int32),
            dma((CHIPS,)),
            dma((2, 2)),
            dma((2, 2, side)),
            dma((2, 2, side)),
            dma((2, 2, 2)),
            dma((2, 2)),
            dma((2, 2, side)),
            dma,
            dma((2,)),
            dma((8, 3)),
            dma((8, 3)),
            dma((CHIPS,)),
            dma((CHIPS,)),
            dma((CHIPS,)),
            dma((CHIPS,)),
            dma((8, 3, HEADS_HERE)),
            dma((8, 3, HEADS_HERE)),
            dma((2, 2)),
            dma((2, 2)),
            dma((2, 2, 2)),
            dma((2, 2, 2)),
            dma((2, side)),
            dma((2, side)),
            dma((8,)),
            dma((8,)),
            dma((8,)),
            dma((8,)),
        ],
        compiler_params=pltpu.CompilerParams(
            collective_id=0, has_side_effects=True, vmem_limit_bytes=60 * 1024 * 1024
        ),
        name="group_backward",
    )(view_counts, view_slots, grad_out, query_act, key_act, value_act, out_proj)
    return pl.pallas_call(
        results,
        out_shape=(gradient, gradient, gradient, jax.ShapeDtypeStruct((piece, width * 8), F32)),
        in_specs=[any_spec] * 4,
        out_specs=(any_spec,) * 4,
        scratch_shapes=[
            pltpu.VMEM((3, rows, width * 8), BF16),
            pltpu.VMEM((8, piece, width), BF16),
            pltpu.VMEM((piece, width * 8), F32),
            dma((7,)),
            dma((7,)),
        ],
        name="results",
    )(*gradients, land)


def results(dq_in, dk_in, dv_in, land_in, dq, dk, dv, gp, held, land, wide, in_sem, out_sem):
    half = dq.shape[0] // 2
    load = [pltpu.make_async_copy(land_in, land, in_sem.at[6])]
    store = [pltpu.make_async_copy(wide, gp, out_sem.at[6])]
    for j, (a, b) in enumerate(((dq_in, dq), (dk_in, dk), (dv_in, dv))):
        for k in range(2):
            part = pl.ds(k * half, half)
            load.append(pltpu.make_async_copy(a.at[part], held.at[j, part], in_sem.at[2 * j + k]))
            store.append(pltpu.make_async_copy(held.at[j, part], b.at[part], out_sem.at[2 * j + k]))
    for copy in load:
        copy.start()
    width = land.shape[2]
    for index in (*range(1, 7), 0):
        load[index].wait()
        if index == 0:
            for source in range(8):
                wide[:, source * width : (source + 1) * width] = land[source].astype(F32)
        store[index].start()
    for copy in store:
        copy.wait()


def solution(mesh):
    rows = P(("dp", "cam"), None)
    in_specs = (rows, rows, rows, rows, P("dp", None), P("dp", None), P("dp", None))
    out_specs = (rows, rows, rows, P("dp", None))
    return jax.shard_map(local, mesh=mesh, in_specs=in_specs, out_specs=out_specs, check_vma=False)
```

```python
import functools
import math

import jax
import jax.numpy as jnp
from jax import lax
from jax.experimental import pallas as pl
from jax.experimental.pallas import tpu as pltpu
from jax.sharding import PartitionSpec as P

HEAD_DIM = 128
VIEW_TOK = 64
HEADS_HERE = 2
CHIPS = 4
BF16 = jnp.bfloat16
F32 = jnp.float32
MESH = pl.DeviceIdType.MESH


def dot(a, b, contract):
    return lax.dot_general(a, b, ((contract[:1], contract[1:]), ((), ())), preferred_element_type=F32)


def kernel(
    dims,
    counts,
    slots,
    g_in,
    q_in,
    k_in,
    v_in,
    w_in,
    dq_out,
    dk_out,
    dv_out,
    land_out,
    g_chip,
    w_all,
    qkv,
    probs,
    att,
    att_send,
    att_recv,
    go_send,
    go_all,
    dk_acc,
    dv_acc,
    d_send,
    gp_send,
    far_recv,
    first_recv,
    second_send,
    second_recv,
    gp_sum,
    line_send,
    line_recv,
    gp_last,
    slot_obj,
    key_obj,
    w_local_sem,
    w_pair_sem,
    w_one_send,
    w_one_recv,
    w_two_send,
    w_pass_send,
    w_two_recv,
    g_local_sem,
    g_sem,
    qkv_recv_sem,
    qkv_send_sem,
    att_send_sem,
    att_recv_sem,
    go_send_sem,
    go_recv_sem,
    d_recv_sem,
    d_send_sem,
    far_send_sem,
    far_recv_sem,
    first_send_sem,
    first_recv_sem,
    second_send_sem,
    second_recv_sem,
    line_send_sem,
    line_recv_sem,
    land_send_sem,
    land_recv_sem,
):
    side, rows, width, piece = dims
    chip_rows = 2 * rows
    tokens = 8 * rows
    model = side * side * 2 * piece
    scale = 1.0 / math.sqrt(HEAD_DIM)
    dp = lax.axis_index("dp")
    cam = lax.axis_index("cam")
    spot, z_lo = dp // 2, dp % 2
    y, x = spot // side, spot % side
    pair = spot * 2 + (1 - z_lo)
    chip, core = cam // 2, cam % 2
    sibling = chip * 2 + (1 - core)
    outs = (dq_out, dk_out, dv_out)
    ins = (q_in, k_in, v_in)

    def block(index):
        return pl.ds(pl.multiple_of(index * rows, rows), rows)

    def chip_block(index):
        return pl.ds(pl.multiple_of(index * chip_rows, chip_rows), chip_rows)

    def cols(index):
        return pl.ds(pl.multiple_of(index * width, width), width)

    def head_cols(index, i):
        return pl.ds(pl.multiple_of(index * width + i * HEAD_DIM, HEAD_DIM), HEAD_DIM)

    def half_piece(index):
        return pl.ds(pl.multiple_of(index * piece, piece), piece)

    def remote(src, dst, send, recv, **where):
        return pltpu.make_async_remote_copy(
            src_ref=src, dst_ref=dst, send_sem=send, recv_sem=recv, device_id=where, device_id_type=MESH
        )

    def arrived(ref, sem):
        pltpu.make_async_copy(ref, ref, sem).wait()

    def at_x(c):
        return (y * side + c) * 2 + z_lo

    def at_y(c):
        return (c * side + x) * 2 + z_lo

    def mine(axis):
        return x if axis == "x" else y

    def other(axis, step):
        return (mine(axis) + step) % side

    def peer(axis, c):
        return at_x(c) if axis == "x" else at_y(c)

    gather_axes = (("y", "x"), ("x", "y"))
    reduce_axes = (("x", "y"), ("y", "x"))

    barrier = pltpu.get_barrier_semaphore()

    def greet(**where):
        pl.semaphore_signal(barrier, inc=1, device_id=where, device_id_type=MESH)

    for step in range(1, side):
        greet(dp=peer("x", other("x", step)))
        greet(dp=peer("y", other("y", step)))
    greet(dp=pair)
    for step in range(1, CHIPS):
        greet(dp=pair, cam=(chip + step) % CHIPS * 2 + core)

    @pl.loop(1, 8)
    def _(step):
        greet(cam=(cam + step) % 8)

    def w_local(c):
        return pltpu.make_async_copy(
            w_in.at[:, cols(c * 2 + core)], w_all.at[c, y, x, half_piece(z_lo), :], w_local_sem.at[c]
        )

    for c in range(CHIPS):
        w_local(c).start()

    def g_local():
        return pltpu.make_async_copy(g_in, g_chip.at[block(core), :], g_local_sem)

    g_local().start()
    pl.semaphore_wait(barrier, 2 * (side - 1) + 1 + (CHIPS - 1) + 7)

    def w_pair_ref(half, z):
        return w_all.at[2 * half : 2 * half + 2, y, x, half_piece(z), :]

    def w_pair(half):
        here = w_pair_ref(half, z_lo)
        there = (chip + half * (CHIPS - 1 + 2 * z_lo)) % CHIPS
        return remote(
            here, here, w_pair_sem.at[0, half], w_pair_sem.at[1, half], dp=pair, cam=there * 2 + core
        )

    def w_one_ref(half, z, c):
        axis = gather_axes[half][0]
        at = (c, x) if axis == "y" else (y, c)
        return w_all.at[2 * half : 2 * half + 2, at[0], at[1], half_piece(z), :]

    def w_one(half, z, step):
        axis = gather_axes[half][0]
        here = w_one_ref(half, z, mine(axis))
        return remote(
            here,
            here,
            w_one_send.at[half, z, step],
            w_one_recv.at[half, z, mine(axis)],
            dp=peer(axis, other(axis, step)),
        )

    def w_two_ref(half, z, c):
        if gather_axes[half][1] == "x":
            return w_all.at[2 * half : 2 * half + 2, :, c, half_piece(z), :]
        return w_all.at[2 * half : 2 * half + 2, c, :, half_piece(z), :]

    def w_two(half, z, way):
        axis = gather_axes[half][1]
        here = w_two_ref(half, z, mine(axis))
        return remote(
            here,
            here,
            w_two_send.at[half, z, way],
            w_two_recv.at[half, z, mine(axis)],
            dp=peer(axis, other(axis, 1 if way == 0 else side - 1)),
        )

    def w_from(half, z):
        return other(gather_axes[half][1], side - 1 + 2 * z)

    def w_pass(half, z):
        axis = gather_axes[half][1]
        here = w_two_ref(half, z, w_from(half, z))
        return remote(
            here,
            here,
            w_pass_send.at[half, z],
            w_two_recv.at[half, z, w_from(half, z)],
            dp=peer(axis, other(axis, side + 1 - 2 * z)),
        )

    def w_two_wait(half, z, c):
        arrived(w_two_ref(half, z, c), w_two_recv.at[half, z, c])

    for c in range(CHIPS):
        w_local(c).wait()
    for half in range(2):
        w_pair(half).start()
    for half in range(2):
        for step in range(1, side):
            w_one(half, z_lo, step).start()

    def qkv_copy(j, step):
        target = (cam + step) % 8
        return remote(
            ins[j].at[:, cols(target)],
            qkv.at[j, block(cam), :],
            qkv_send_sem.at[step, j],
            qkv_recv_sem.at[cam, j],
            cam=target,
        )

    def qkv_start(j):
        @pl.loop(1, 8)
        def _(step):
            qkv_copy(j, step).start()

        pltpu.make_async_copy(
            ins[j].at[:, cols(cam)], qkv.at[j, block(cam), :], qkv_recv_sem.at[cam, j]
        ).start()

    qkv_start(0)

    g_copy = remote(g_in, g_chip.at[block(core), :], g_sem.at[0], g_sem.at[1], cam=sibling)
    g_copy.start()

    for half in range(2):
        arrived(w_pair_ref(half, 1 - z_lo), w_pair_sem.at[1, half])
        for step in range(1, side):
            w_one(half, 1 - z_lo, step).start()
    qkv_start(1)

    ends = [counts[0, 0]]
    for o in range(1, counts.shape[1]):
        ends.append(ends[-1] + counts[0, o])
    views = slots.shape[1]
    view_obj = [sum((v >= end).astype(jnp.int32) for end in ends) for v in range(views)]

    @pl.loop(0, views)
    def _(s):
        found = jnp.int32(0)
        for v in range(views):
            found = found + jnp.where(slots[0, v] == s, view_obj[v], 0)
        slot_obj[s] = found

    lane_slot = lax.broadcasted_iota(jnp.int32, (1, tokens), 1) // VIEW_TOK
    lane_obj = jnp.zeros((1, tokens), jnp.int32)
    for s in range(views):
        lane_obj = jnp.where(lane_slot == s, slot_obj[s], lane_obj)
    key_obj[...] = lane_obj
    dk_acc[...] = jnp.zeros_like(dk_acc)
    dv_acc[...] = jnp.zeros_like(dv_acc)

    def qkv_wait(j):
        @pl.loop(0, 8)
        def _(source):
            arrived(qkv.at[j, block(source), :], qkv_recv_sem.at[source, j])

    for z in (z_lo, 1 - z_lo):
        for half in range(2):
            axis = gather_axes[half][0]
            for step in range(1, side):
                c = other(axis, step)
                arrived(w_one_ref(half, z, c), w_one_recv.at[half, z, c])
            for way in range(2):
                w_two(half, z, way).start()
    qkv_wait(0)
    qkv_start(2)
    qkv_wait(1)

    def att_copy(c):
        return remote(
            att_send.at[chip_block(c), :],
            att_recv.at[:, cols(chip)],
            att_send_sem.at[c],
            att_recv_sem.at[chip],
            cam=c * 2 + core,
        )

    def nth(u, first, second, third, fourth):
        return jnp.where(u == 0, first, jnp.where(u == 1, second, jnp.where(u == 2, third, fourth)))

    @pl.loop(0, CHIPS)
    def _(u):
        c = (chip + nth(u, 2, 1, 3, 0)) % CHIPS

        @pl.loop(0, 2)
        def _(k):
            r = c * 2 + k
            here = block(r)
            row = lax.broadcasted_iota(jnp.int32, (rows, 1), 0)
            row_obj = jnp.where(row < VIEW_TOK, slot_obj[r * 2], slot_obj[r * 2 + 1])
            same = row_obj == key_obj[...]
            for i in range(HEADS_HERE):
                head = slice(i * HEAD_DIM, (i + 1) * HEAD_DIM)
                scores = dot(qkv[0, here, head], qkv[1, :, head], (1, 1)) * scale
                scores = jnp.where(same, scores, -jnp.inf)
                exps = jnp.exp(scores - jnp.max(scores, axis=1, keepdims=True))
                p = exps * (1.0 / jnp.sum(exps, axis=1, keepdims=True))
                probs[i, here, :] = p

    qkv_wait(2)

    @pl.loop(0, CHIPS)
    def _(u):
        c = (chip + nth(u, 2, 1, 3, 0)) % CHIPS
        there = chip_block(c)
        for i in range(HEADS_HERE):
            head = slice(i * HEAD_DIM, (i + 1) * HEAD_DIM)
            att[there, head] = dot(probs[i, there, :].astype(BF16), qkv[2, :, head], (1, 0))

        @pl.when(u < CHIPS - 1)
        def _():
            att_send[there, :] = att[there, :].astype(BF16)
            att_copy(c).start()

        @pl.when(u == CHIPS - 1)
        def _():
            att_recv[:, cols(chip)] = att[there, :].astype(BF16)

        @pl.when(u < 2)
        def _():
            z = jnp.where(u == 0, z_lo, 1 - z_lo)
            for half in range(2):
                w_two_wait(half, z, w_from(half, z))
                w_pass(half, z).start()

    g_local().wait()
    arrived(g_chip.at[block(1 - core), :], g_sem.at[1])

    for half in range(2):
        axis = gather_axes[half][1]
        for z in range(2):
            w_two_wait(half, z, other(axis, 1 + (side - 2) * z))
            for step in range(2, side - 1):
                w_two_wait(half, z, other(axis, step))
    def go_copy(c):
        return remote(
            go_send.at[c], go_all.at[chip_block(chip), :], go_send_sem.at[c], go_recv_sem.at[chip], cam=c * 2 + core
        )

    @pl.loop(0, CHIPS)
    def _(u):
        c = (chip + nth(u, 2, 1, 3, 0)) % CHIPS
        grad_att = dot(g_chip[...], w_all[c].reshape(model, width), (1, 0)).astype(BF16)

        @pl.when(u < CHIPS - 1)
        def _():
            go_send[c] = grad_att
            go_copy(c).start()

        @pl.when(u == CHIPS - 1)
        def _():
            go_all[chip_block(chip), :] = grad_att

    for step in range(1, CHIPS):
        c = (chip + step) % CHIPS
        arrived(att_recv.at[:, cols(c)], att_recv_sem.at[c])

    def first_part(half, part, c):
        if reduce_axes[half][0] == "x":
            return gp_send.at[2 * half + part, :, c]
        return gp_send.at[2 * half + part, c]

    def toward(half, part):
        return other(reduce_axes[half][0], 1 if part == 0 else side - 1)

    def far_copy(half, part):
        axis = reduce_axes[half][0]
        return remote(
            first_part(half, part, other(axis, 2)),
            far_recv.at[half, part],
            far_send_sem.at[half, part],
            far_recv_sem.at[half, part],
            dp=peer(axis, toward(half, part)),
        )

    def first_copy(half, way, part):
        return remote(
            first_part(half, part, toward(half, way)),
            first_recv.at[half, way, part],
            first_send_sem.at[half, way, part],
            first_recv_sem.at[half, way, part],
            dp=peer(reduce_axes[half][0], toward(half, way)),
        )

    for half in range(2):
        att_half = att_recv[:, 2 * half * width : 2 * (half + 1) * width]

        @pl.loop(0, side * side // 2)
        def _(j):
            tile = pl.ds(pl.multiple_of(j * 4 * piece, 128), 4 * piece)
            total = dot(g_chip[:, tile], att_half, (0, 0)).astype(BF16)
            for s in range(2):
                for c in range(2):
                    gp_send[2 * half + c, (2 * j + s) // side, (2 * j + s) % side] = total[
                        s * 2 * piece : (s + 1) * 2 * piece, c * width : (c + 1) * width
                    ]

        for part in range(2):
            far_copy(half, part).start()

    for half in range(2):
        for part in range(2):
            first_copy(half, 1 - part, part).start()

    def d_copy(j, i, target):
        return remote(
            d_send.at[j, block(target), i * HEAD_DIM : (i + 1) * HEAD_DIM],
            outs[j].at[:, head_cols(cam, i)],
            d_send_sem.at[target, j, i],
            d_recv_sem.at[cam, j, i],
            cam=target,
        )

    def d_local(j, i):
        return pltpu.make_async_copy(
            d_send.at[j, block(cam), i * HEAD_DIM : (i + 1) * HEAD_DIM],
            outs[j].at[:, head_cols(cam, i)],
            d_recv_sem.at[cam, j, i],
        )

    def backward(c, i):
        here = chip_block(c)
        head = slice(i * HEAD_DIM, (i + 1) * HEAD_DIM)
        go = go_all[here, head]
        p = probs[i, here, :]
        delta = jnp.sum(go.astype(F32) * att[here, head], axis=1, keepdims=True)
        ds = (p * (dot(go, qkv[2, :, head], (1, 1)) - delta)).astype(BF16)
        d_send[0, here, head] = (dot(ds, qkv[1, :, head], (1, 0)) * scale).astype(BF16)
        dk_acc[:, head] += dot(ds, qkv[0, here, head], (0, 0))
        dv_acc[:, head] += dot(p.astype(BF16), go, (0, 0))

    for i in range(HEADS_HERE):
        backward(chip, i)
        d_local(0, i).start()
        d_copy(0, i, sibling).start()

    for i in range(HEADS_HERE):
        head = slice(i * HEAD_DIM, (i + 1) * HEAD_DIM)

        @pl.loop(1, CHIPS)
        def _(t):
            c = (chip + nth(t, 0, 3, 1, 2)) % CHIPS
            if i == 0:
                arrived(go_all.at[chip_block(c), :], go_recv_sem.at[c])

                @pl.when(t == 2)
                def _():
                    for half in range(2):
                        for part in range(2):
                            arrived(far_recv.at[half, part], far_recv_sem.at[half, part])
                            own = first_part(half, part, toward(half, part))
                            own[...] = (own[...].astype(F32) + far_recv[half, part].astype(F32)).astype(BF16)
                            first_copy(half, part, part).start()

            backward(c, i)
            d_copy(0, i, c * 2).start()
            d_copy(0, i, c * 2 + 1).start()

        d_send[1, :, head] = (dk_acc[:, head] * scale).astype(BF16)
        d_send[2, :, head] = dv_acc[:, head].astype(BF16)
        for j in range(1, 3):

            @pl.loop(1, 8)
            def _(step):
                d_copy(j, i, (cam + step) % 8).start()

            d_local(j, i).start()

    def second_copy(half, step):
        axis = reduce_axes[half][1]
        c = other(axis, step)
        return remote(
            second_send.at[half, c],
            second_recv.at[half, mine(axis)],
            second_send_sem.at[half, step],
            second_recv_sem.at[half, mine(axis)],
            dp=peer(axis, c),
        )

    for half in range(2):
        axis, later = reduce_axes[half]
        for way in range(2):
            for part in range(2):
                arrived(first_recv.at[half, way, part], first_recv_sem.at[half, way, part])

        def partial(i):
            own = (slice(2 * half, 2 * half + 2), i, x) if axis == "x" else (slice(2 * half, 2 * half + 2), y, i)
            total = gp_send[own].astype(F32)
            for way in range(2):
                total = total + first_recv[half, way, :, i].astype(F32)
            return total

        for step in range(1, side):
            i = other(later, step)
            second_send[half, i] = partial(i).astype(BF16)
            second_copy(half, step).start()
        gp_sum[2 * half : 2 * half + 2] = partial(mine(later))

    for half in range(2):
        later = reduce_axes[half][1]
        for step in range(1, side):
            c = other(later, step)
            arrived(second_recv.at[half, c], second_recv_sem.at[half, c])
            gp_sum[2 * half : 2 * half + 2] += second_recv[half, c].astype(F32)

    line_send[...] = gp_sum[...].astype(BF16)
    here_z = chip * 2 + z_lo

    def line_copy(step):
        target = (here_z + step) % 8
        return remote(
            line_send.at[target // 2, half_piece(target % 2), :],
            line_recv.at[here_z],
            line_send_sem.at[step],
            line_recv_sem.at[here_z],
            dp=spot * 2 + target % 2,
            cam=target // 2 * 2 + core,
        )

    @pl.loop(1, 8)
    def _(step):
        line_copy(step).start()

    total = gp_sum[chip, half_piece(z_lo), :]
    for step in range(1, 8):
        source = (here_z + 8 - step) % 8
        arrived(line_recv.at[source], line_recv_sem.at[source])
        total = total + line_recv[source].astype(F32)
    gp_last[...] = total.astype(BF16)

    def land_copy(step):
        target = (chip + step) % CHIPS * 2 + core if step else sibling
        return remote(gp_last, land_out.at[cam], land_send_sem.at[step], land_recv_sem.at[cam], cam=target)

    def land_pass(step):
        source = (chip + step) % CHIPS * 2 + core
        here = land_out.at[source]
        return remote(here, here, land_send_sem.at[CHIPS + step], land_recv_sem.at[source], cam=sibling)

    for step in (2, 1, 3, 0):
        land_copy(step).start()
    pltpu.make_async_copy(gp_last, land_out.at[cam], land_recv_sem.at[cam]).start()
    for step in (1, 3, 2):
        source = (chip + step) % CHIPS * 2 + core
        arrived(land_out.at[source], land_recv_sem.at[source])
        land_pass(step).start()

    for j in range(3):

        @pl.loop(0, 8)
        def _(source):
            for i in range(HEADS_HERE):
                arrived(outs[j].at[:, head_cols(source, i)], d_recv_sem.at[source, j, i])

    arrived(land_out.at[cam], land_recv_sem.at[cam])
    for step in range(CHIPS):
        source = (chip + step) % CHIPS * 2 + 1 - core
        arrived(land_out.at[source], land_recv_sem.at[source])

    for half in range(2):
        w_pair(half).wait_send()
    g_copy.wait_send()
    for half in range(2):
        for step in range(1, side):
            for z in range(2):
                w_one(half, z, step).wait_send()
            second_copy(half, step).wait_send()
        for z in range(2):
            w_pass(half, z).wait_send()
            far_copy(half, z).wait_send()
            for part in range(2):
                first_copy(half, z, part).wait_send()
            for way in range(2):
                w_two(half, z, way).wait_send()
    for step in range(1, CHIPS):
        c = (chip + step) % CHIPS
        att_copy(c).wait_send()
        go_copy(c).wait_send()

    @pl.loop(1, 8)
    def _(step):
        for j in range(3):
            qkv_copy(j, step).wait_send()
            for i in range(HEADS_HERE):
                d_copy(j, i, (cam + step) % 8).wait_send()
        line_copy(step).wait_send()

    for step in range(CHIPS):
        land_copy(step).wait_send()
        if step:
            land_pass(step).wait_send()


def local(grad_out, query_act, key_act, value_act, out_proj, view_counts, view_slots):
    rows, model = grad_out.shape
    planes = lax.axis_size("dp") // 2
    side = math.isqrt(planes)
    piece = out_proj.shape[0]
    width = query_act.shape[1] // 8
    tokens = rows * 8
    dims = (side, rows, width, piece)
    any_spec = pl.BlockSpec(memory_space=pl.ANY)
    dma = pltpu.SemaphoreType.DMA
    gradient = jax.ShapeDtypeStruct(query_act.shape, BF16)
    *gradients, land = pl.pallas_call(
        functools.partial(kernel, dims),
        out_shape=(gradient, gradient, gradient, jax.ShapeDtypeStruct((8, piece, width), BF16)),
        in_specs=[pl.BlockSpec(memory_space=pltpu.SMEM)] * 2 + [any_spec] * 5,
        out_specs=(any_spec,) * 4,
        scratch_shapes=[
            pltpu.VMEM((2 * rows, model), BF16),
            pltpu.VMEM((CHIPS, side, side, 2 * piece, width), BF16),
            pltpu.VMEM((3, tokens, width), BF16),
            pltpu.VMEM((HEADS_HERE, tokens, tokens), F32),
            pltpu.VMEM((tokens, width), F32),
            pltpu.VMEM((tokens, width), BF16),
            pltpu.VMEM((2 * rows, CHIPS * width), BF16),
            pltpu.VMEM((CHIPS, 2 * rows, width), BF16),
            pltpu.VMEM((tokens, width), BF16),
            pltpu.VMEM((tokens, width), F32),
            pltpu.VMEM((tokens, width), F32),
            pltpu.VMEM((3, tokens, width), BF16),
            pltpu.VMEM((CHIPS, side, side, 2 * piece, width), BF16),
            pltpu.VMEM((2, 2, side, 2 * piece, width), BF16),
            pltpu.VMEM((2, 2, 2, side, 2 * piece, width), BF16),
            pltpu.VMEM((2, side, 2, 2 * piece, width), BF16),
            pltpu.VMEM((2, side, 2, 2 * piece, width), BF16),
            pltpu.VMEM((CHIPS, 2 * piece, width), F32),
            pltpu.VMEM((CHIPS, 2 * piece, width), BF16),
            pltpu.VMEM((8, piece, width), BF16),
            pltpu.VMEM((piece, width), BF16),
            pltpu.SMEM((view_slots.shape[1],), jnp.int32),
            pltpu.VMEM((1, tokens), jnp.int32),
            dma((CHIPS,)),
            dma((2, 2)),
            dma((2, 2, side)),
            dma((2, 2, side)),
            dma((2, 2, 2)),
            dma((2, 2)),
            dma((2, 2, side)),
            dma,
            dma((2,)),
            dma((8, 3)),
            dma((8, 3)),
            dma((CHIPS,)),
            dma((CHIPS,)),
            dma((CHIPS,)),
            dma((CHIPS,)),
            dma((8, 3, HEADS_HERE)),
            dma((8, 3, HEADS_HERE)),
            dma((2, 2)),
            dma((2, 2)),
            dma((2, 2, 2)),
            dma((2, 2, 2)),
            dma((2, side)),
            dma((2, side)),
            dma((8,)),
            dma((8,)),
            dma((8,)),
            dma((8,)),
        ],
        compiler_params=pltpu.CompilerParams(
            collective_id=0, has_side_effects=True, vmem_limit_bytes=60 * 1024 * 1024
        ),
        name="group_backward",
    )(view_counts, view_slots, grad_out, query_act, key_act, value_act, out_proj)
    return pl.pallas_call(
        results,
        out_shape=(gradient, gradient, gradient, jax.ShapeDtypeStruct((piece, width * 8), F32)),
        in_specs=[any_spec] * 4,
        out_specs=(any_spec,) * 4,
        scratch_shapes=[
            pltpu.VMEM((3, rows, width * 8), BF16),
            pltpu.VMEM((8, piece, width), BF16),
            pltpu.VMEM((piece, width * 8), F32),
            dma((7,)),
            dma((7,)),
        ],
        name="results",
    )(*gradients, land)


def results(dq_in, dk_in, dv_in, land_in, dq, dk, dv, gp, held, land, wide, in_sem, out_sem):
    half = dq.shape[0] // 2
    load = [pltpu.make_async_copy(land_in, land, in_sem.at[6])]
    store = [pltpu.make_async_copy(wide, gp, out_sem.at[6])]
    for j, (a, b) in enumerate(((dq_in, dq), (dk_in, dk), (dv_in, dv))):
        for k in range(2):
            part = pl.ds(k * half, half)
            load.append(pltpu.make_async_copy(a.at[part], held.at[j, part], in_sem.at[2 * j + k]))
            store.append(pltpu.make_async_copy(held.at[j, part], b.at[part], out_sem.at[2 * j + k]))
    for copy in load:
        copy.start()
    width = land.shape[2]
    for index in (*range(1, 7), 0):
        load[index].wait()
        if index == 0:
            for source in range(8):
                wide[:, source * width : (source + 1) * width] = land[source].astype(F32)
        store[index].start()
    for copy in store:
        copy.wait()


def solution(mesh):
    rows = P(("dp", "cam"), None)
    in_specs = (rows, rows, rows, rows, P("dp", None), P("dp", None), P("dp", None))
    out_specs = (rows, rows, rows, P("dp", None))
    return jax.shard_map(local, mesh=mesh, in_specs=in_specs, out_specs=out_specs, check_vma=False)
```
